128 devices in a mesh: section: 2 (over core), dp: 64 (over y, z, x).
Axes of the slice: x: 4, y: 4, z: 4, core: 2. Of those that a mesh axis runs over, the one named last changes fastest.
Arguments:
- inputs: bfloat16 [2, 4096, 960], P(None, 'dp'), may hold values from -16 to 16
- starts: int32 [2, 4096], P(None, 'dp'), may hold values from 0 to 64, as said below
- cotangent: bfloat16 [2, 4096, 960], P(None, 'dp'), may hold values from -16 to 16
- w_query: bfloat16 [2, 960, 960], P('section', 'dp'), may hold values from -0.1875 to 0.1875
- w_key: bfloat16 [2, 960, 320], P('section', 'dp'), may hold values from -0.1875 to 0.1875
- w_value: bfloat16 [2, 960, 320], P('section', 'dp'), may hold values from -0.1875 to 0.1875
- w_output: bfloat16 [2, 960, 960], P('section', 'dp'), may hold values from -0.75 to 0.75
- w_gate: bfloat16 [2, 960, 2560], P('section', 'dp'), may hold values from -0.1875 to 0.1875
- w_up: bfloat16 [2, 960, 2560], P('section', 'dp'), may hold values from -0.1875 to 0.1875
- w_down: bfloat16 [2, 2560, 960], P('section', 'dp'), may hold values from -0.15625 to 0.15625
- attn_gain: bfloat16 [2, 960], P('section', 'dp'), may hold values from 0.25 to 1.75
- ffn_gain: bfloat16 [2, 960], P('section', 'dp'), may hold values from 0.25 to 1.75
Outputs:
- activations: bfloat16 [2, 2, 4096, 960], P('section', None, 'dp')
- input_grads: bfloat16 [2, 2, 4096, 960], P('section', None, 'dp')
- grad_query: float32 [2, 960, 960], P('section', 'dp')
- grad_key: float32 [2, 960, 320], P('section', 'dp')
- grad_value: float32 [2, 960, 320], P('section', 'dp')
- grad_output: float32 [2, 960, 960], P('section', 'dp')
- grad_gate: float32 [2, 960, 2560], P('section', 'dp')
- grad_up: float32 [2, 960, 2560], P('section', 'dp')
- grad_down: float32 [2, 2560, 960], P('section', 'dp')
- grad_attn_gain: float32 [2, 960], P('section', 'dp')
- grad_ffn_gain: float32 [2, 960], P('section', 'dp')
The draws below stay inside these ranges and needn't reach their ends.
Inputs may be any that keep to these rules, and one draw needn't show every extreme that they name: `starts`: within each aligned block of 64 rows (one index of dp, one micro-batch) sequences lie end to end from the block's first row, each row holding the block-local index of its sequence's first row; the rows after the last sequence are padding and hold 64. At least a quarter of every block's rows are in sequences, and some blocks are full.
All inputs are finite; a program needn't handle non-finite values.
Results may differ from the reference program's by a relative error of at most 0.023.
Values may be sent and summed in bfloat16 or wider, within the bound.
No kernel may reach another device: no remote copies, remote signals or barrier semaphores. Data moves between devices by JAX's collectives and lax.ppermute only.
A program may use at most 256 MiB of HBM per device.

```python
from functools import partial
import jax
import jax.numpy as jnp
from jax import lax

D = 960
HEADS = 15
KV_HEADS = 5
HEAD_DIM = 64
FF = 2560
CAP = 64
MICRO = 2
QD = 960
KVD = 320
TOKENS = 4096
N_SECTION = 2


def draw_starts(key, part):
    blocks = MICRO * (TOKENS // CAP)
    key_fill = jax.random.fold_in(key, 101)
    key_whole = jax.random.fold_in(key, 202)
    key_mark = jax.random.fold_in(key, 303)
    filled = jax.random.randint(key_fill, (blocks, 1), CAP // 4, CAP, dtype=jnp.int32)
    whole_block = jax.random.randint(key_whole, (blocks, 1), 0, 3, dtype=jnp.int32) == 0
    block_ids = jnp.arange(blocks, dtype=jnp.int32)[:, None]
    filled = jnp.where(whole_block | (block_ids == 0), CAP, filled)
    rows_idx = jnp.arange(CAP, dtype=jnp.int32)[None, :]
    new_seq = jax.random.randint(key_mark, (blocks, CAP), 0, max(CAP // 4, 2), dtype=jnp.int32) == 0
    new_seq = new_seq | (rows_idx == 0)
    begins = lax.cummax(jnp.where(new_seq, rows_idx, 0), axis=1)
    result = jnp.where(rows_idx < filled, begins, CAP)
    return result.reshape(MICRO, TOKENS).astype(jnp.int32)


def with_spikes(array, rng, source, target, blocks, factor):
    def block_of(dim):
        return (jnp.arange(array.shape[dim]) // (array.shape[dim] // blocks)).reshape((-1,) + (1,) * (array.ndim - 1 - dim))

    first = jax.random.permutation(rng, blocks)[block_of(target)]
    other_side = (block_of(target) + blocks // 2) % blocks
    return jnp.where((block_of(source) == first) | (block_of(source) == other_side), factor * array, array)


def block_scale(rng, extent, split, low, largest):
    level = 1.0
    for dim, parts in split:
        steps = jax.random.uniform(jax.random.fold_in(jax.random.fold_in(rng, 6), dim), (parts,), jnp.float32, low / len(split), largest / len(split))
        level = level * jnp.repeat(jnp.exp(steps), extent[dim] // parts).reshape((-1,) + (1,) * (len(extent) - 1 - dim))
    return level


def gaussian(stream_key, shape, scale, reach, pieces=(), kind=jnp.bfloat16):
    array = scale * jax.random.normal(stream_key, shape, jnp.float32)
    if pieces:
        array = array * block_scale(stream_key, shape, pieces, -0.22, 0.18)
    return jnp.clip(array, -reach, reach).astype(kind)


def bell_draw_with(rng, dims, width, most, pieces, heavy, kind=jnp.bfloat16):
    drawn = width * jax.random.normal(rng, dims, jnp.float32)
    if pieces:
        drawn = drawn * block_scale(rng, dims, pieces, -0.22, 0.18)
    return jnp.clip(with_spikes(drawn, jax.random.fold_in(rng, 3), *heavy), -most, most).astype(kind)


def setup_inputs(seed: int = 0) -> dict:
    key_list = jax.random.split(jax.random.key(seed), 13)
    return {
        "inputs": bell_draw_with(key_list[0], (MICRO, TOKENS, D), 1.0, 16.0, ((1, 64),), (1, 2, 64, 4.0)),
        "starts": draw_starts(jax.random.fold_in(key_list[12], 71), 0),
        "cotangent": bell_draw_with(key_list[2], (MICRO, TOKENS, D), 1.0, 16.0, ((1, 64),), (1, 2, 64, 4.0)),
        "w_query": gaussian(key_list[3], (N_SECTION, D, QD), D ** -0.5, 0.1875, ((0, 2), (1, 64))),
        "w_key": gaussian(key_list[4], (N_SECTION, D, KVD), D ** -0.5, 0.1875, ((0, 2), (1, 64))),
        "w_value": gaussian(key_list[5], (N_SECTION, D, KVD), D ** -0.5, 0.1875, ((0, 2), (1, 64))),
        "w_output": gaussian(key_list[6], (N_SECTION, QD, D), (D // 16) ** -0.5, 0.75, ((0, 2), (1, 64))),
        "w_gate": gaussian(key_list[7], (N_SECTION, D, FF), D ** -0.5, 0.1875, ((0, 2), (1, 64))),
        "w_up": gaussian(key_list[8], (N_SECTION, D, FF), D ** -0.5, 0.1875, ((0, 2), (1, 64))),
        "w_down": gaussian(key_list[9], (N_SECTION, FF, D), (FF // 2) ** -0.5, 0.15625, ((0, 2), (1, 64))),
        "attn_gain": jnp.clip(1.0 + 0.15 * jax.random.normal(key_list[10], (N_SECTION, D), jnp.float32), 0.25, 1.75).astype(jnp.bfloat16),
        "ffn_gain": jnp.clip(1.0 + 0.15 * jax.random.normal(key_list[11], (N_SECTION, D), jnp.float32), 0.25, 1.75).astype(jnp.bfloat16),
    }


@jax.custom_vjp
def low(v):
    return lax.optimization_barrier(v.astype(jnp.bfloat16)).astype(jnp.float32)

@jax.custom_vjp
def low_back(v):
    return v

def low_keep(v):
    return (low(v), None)

def low_pass(kept, grad):
    return (grad,)

def back_keep(v):
    return (v, None)

def back_low(kept, grad):
    return (low(grad),)
low.defvjp(low_keep, low_pass)
low_back.defvjp(back_keep, back_low)
norm_eps = 1e-05
masked_score = -1e+30
rope_base = 10000.0

def exact_dot(left, right):
    return jnp.dot(left, right, preferred_element_type=jnp.float32, precision=lax.Precision.HIGHEST)

def rms_scale(values, gain):
    inverse = lax.rsqrt(lax.optimization_barrier(jnp.mean(values * values, axis=-1, keepdims=True)) + norm_eps)
    return values * inverse * gain

def rotate(values, cosine_table, sine_table):
    half_dim = values.shape[-1] // 2
    first_half = values[..., :half_dim]
    second_half = values[..., half_dim:]
    return jnp.concatenate([first_half * cosine_table - second_half * sine_table, second_half * cosine_table + first_half * sine_table], axis=-1)

def swiglu(gate_vals, up_vals):
    return jax.nn.silu(gate_vals) * up_vals

def layer(source, weights, starts):
    w_query, w_key, w_value, w_output, w_gate, w_up, w_down, attn_gain, ffn_gain = weights
    total_rows = source.shape[0]
    blocks = total_rows // CAP
    group_size = HEADS // KV_HEADS
    local_rows = jnp.arange(total_rows, dtype=jnp.int32) % CAP
    live_mask = starts <= local_rows
    live_rows = live_mask.astype(jnp.float32)[:, None]
    position = jnp.where(live_mask, local_rows - starts, 0).astype(jnp.float32)
    frequency = rope_base ** (-2.0 * jnp.arange(HEAD_DIM // 2, dtype=jnp.float32) / HEAD_DIM)
    angles = position[:, None, None] * frequency[None, None, :]
    cosine_table = jnp.cos(angles)
    sine_table = jnp.sin(angles)
    normed = low(rms_scale(source, attn_gain))
    query_raw = low_back(exact_dot(normed, w_query))
    key_raw = low_back(exact_dot(normed, w_key))
    value_low = low(low_back(exact_dot(normed, w_value)))
    query_rot = low(rotate(query_raw.reshape(total_rows, HEADS, HEAD_DIM), cosine_table, sine_table))
    key_rot = low(rotate(key_raw.reshape(total_rows, KV_HEADS, HEAD_DIM), cosine_table, sine_table))
    grouped = query_rot.reshape(blocks, CAP, KV_HEADS, group_size, HEAD_DIM)
    key_blocks = key_rot.reshape(blocks, CAP, KV_HEADS, HEAD_DIM)
    value_blocks = value_low.reshape(blocks, CAP, KV_HEADS, HEAD_DIM)
    scores = jnp.einsum('bqhgd,bkhd->bhgqk', grouped, key_blocks, precision=lax.Precision.HIGHEST)
    scores = low_back(scores * HEAD_DIM ** (-0.5))
    block_starts = starts.reshape(blocks, CAP)
    block_local = jnp.arange(CAP, dtype=jnp.int32)
    causal = block_local[None, None, :] <= block_local[None, :, None]
    inside = block_local[None, None, :] >= block_starts[:, :, None]
    diagonal = (block_local[None, :] == block_local[:, None])[None]
    allowed = causal & inside | diagonal
    scores = jnp.where(allowed[:, None, None], scores, masked_score)
    attn_probs = low(jax.nn.softmax(scores, axis=-1))
    attn_mixed = jnp.einsum('bhgqk,bkhd->bqhgd', attn_probs, value_blocks, precision=lax.Precision.HIGHEST)
    attn_mixed = low(low_back(attn_mixed.reshape(total_rows, HEADS * HEAD_DIM)))
    middle = source + low_back(exact_dot(attn_mixed, w_output))
    second = low(rms_scale(middle, ffn_gain))
    gate_vals = low_back(exact_dot(second, w_gate))
    up_vals = low_back(exact_dot(second, w_up))
    hidden = low(swiglu(gate_vals, up_vals))
    result = (middle + low_back(exact_dot(hidden, w_down))) * live_rows
    return low(low_back(result))

def reference(inputs, starts, cotangent, w_query, w_key, w_value, w_output, w_gate, w_up, w_down, attn_gain, ffn_gain):
    params = tuple((matrix.astype(jnp.float32) for matrix in (w_query, w_key, w_value, w_output, w_gate, w_up, w_down, attn_gain, ffn_gain)))
    section_params = [tuple((matrix[section_idx] for matrix in params)) for section_idx in range(N_SECTION)]
    section_totals = [[jnp.zeros_like(matrix) for matrix in section_params[section_idx]] for section_idx in range(N_SECTION)]
    acts_list = []
    grads_list = []
    for micro_idx in range(MICRO):
        starts_now = starts[micro_idx]
        current = inputs[micro_idx].astype(jnp.float32)
        backers = []
        outputs_now = []
        for section_idx in range(N_SECTION):
            current, backer = jax.vjp(partial(layer, starts=starts_now), current, section_params[section_idx])
            backers.append(backer)
            outputs_now.append(current)
        flowing = cotangent[micro_idx].astype(jnp.float32)
        grads_now = [None] * N_SECTION
        for section_idx in reversed(range(N_SECTION)):
            flowing, weight_grads = backers[section_idx](flowing)
            grads_now[section_idx] = flowing
            section_totals[section_idx] = [old_sum + new_sum for old_sum, new_sum in zip(section_totals[section_idx], weight_grads)]
        acts_list.append(jnp.stack(outputs_now))
        grads_list.append(jnp.stack(grads_now))
    activations = jnp.stack(acts_list, axis=1).astype(jnp.bfloat16)
    input_grads = jnp.stack(grads_list, axis=1).astype(jnp.bfloat16)
    stacked = [jnp.stack([section_totals[section_idx][member] for section_idx in range(N_SECTION)]) for member in range(9)]
    return (activations, input_grads, stacked[0], stacked[1], stacked[2], stacked[3], stacked[4], stacked[5], stacked[6], stacked[7], stacked[8])
```

```python
import jax
import jax.numpy as jnp
from jax import lax
from jax.sharding import PartitionSpec as P

D = 960
HEADS = 15
KV_HEADS = 5
GROUP = HEADS // KV_HEADS
HEAD_DIM = 64
FF = 2560
QD = 960
KVD = 320
OWNERS = 64
SLOT = 15
PADDED = 16
DOWN_ROWS = 40

norm_eps = 1e-05
masked_score = -1e30
rope_base = 10000.0

f32 = jnp.float32
bf16 = jnp.bfloat16


def gray(value):
    return value ^ (value >> 1)


AXIS_SHIFT = {"y": 4, "z": 2, "x": 0}
BITS = (("y", 1), ("y", 0), ("z", 1), ("z", 0), ("x", 1), ("x", 0))


def partner_pairs(bit):
    axis, place = bit
    shift = AXIS_SHIFT[axis]
    pairs = []
    for source in range(OWNERS):
        coordinate = (source >> shift) & 3
        other = gray(gray(coordinate) ^ (1 << place))
        pairs.append((source, source + ((other - coordinate) << shift)))
    return pairs


def owner_of(position):
    me = lax.axis_index("dp")
    owner = 0
    for shift in (4, 2, 0):
        owner = owner + (gray(gray((me >> shift) & 3) ^ ((position >> shift) & 3)) << shift)
    return owner


def dot(left, right):
    return jnp.dot(left, right, preferred_element_type=f32)


def dot_t(left, right):
    return lax.dot_general(left, right, (((1,), (1,)), ((), ())), preferred_element_type=f32)


def spread_matrix():
    row = lax.broadcasted_iota(jnp.int32, (D, OWNERS * PADDED), 0)
    col = lax.broadcasted_iota(jnp.int32, (D, OWNERS * PADDED), 1)
    return ((row == SLOT * (col // PADDED) + col % PADDED) & (col % PADDED < SLOT)).astype(bf16)


def own_spread():
    row = lax.broadcasted_iota(jnp.int32, (OWNERS * PADDED, D), 0)
    col = lax.broadcasted_iota(jnp.int32, (OWNERS * PADDED, D), 1)
    owner = owner_of(row // PADDED)
    return ((col == SLOT * owner + row % PADDED) & (row % PADDED < SLOT)).astype(bf16)


def gather_rows(values, spread):
    high = values.astype(bf16)
    low = (values - high.astype(f32)).astype(bf16)
    return dot_t(high, spread) + dot_t(low, spread)


def geometry(starts):
    rows = starts.shape[-1]
    local = jnp.arange(rows, dtype=jnp.int32)
    live = starts <= local
    position = jnp.where(live, local - starts, 0).astype(f32)
    frequency = rope_base ** (-2.0 * jnp.arange(HEAD_DIM // 2, dtype=f32) / HEAD_DIM)
    angles = position[..., None, None] * frequency
    causal = local[None, :] <= local[:, None]
    inside = local >= starts[..., None]
    diagonal = local[None, :] == local[:, None]
    allowed = causal & inside | diagonal
    return live.astype(f32).reshape(-1, 1), jnp.cos(angles), jnp.sin(angles), allowed


def rotate(values, cosine, sine):
    half = HEAD_DIM // 2
    first, second = values[..., :half], values[..., half:]
    return jnp.concatenate(
        [first * cosine - second * sine, second * cosine + first * sine], axis=-1
    )


def norm_parts(values):
    inverse = lax.rsqrt(jnp.mean(values * values, axis=-1, keepdims=True) + norm_eps)
    return values * inverse, inverse


def norm_back(grad, normal, inverse, gain):
    scaled = grad * gain
    return inverse * (scaled - normal * jnp.mean(scaled * normal, axis=-1, keepdims=True))


def forward(source, weights, geo, spread):
    w_query, w_key, w_value, w_output, w_gate, w_up, w_down, attn_gain, ffn_gain = weights
    live, cosine, sine, allowed = geo
    micro, rows = cosine.shape[:2]
    h = source.astype(f32)
    n1, r1 = norm_parts(h)
    a = (n1 * attn_gain).astype(bf16)
    a_wide = dot(a, spread).astype(bf16)
    q = rotate(dot(a_wide, w_query).reshape(micro, rows, HEADS, HEAD_DIM), cosine, sine)
    k = rotate(dot(a_wide, w_key).reshape(micro, rows, KV_HEADS, HEAD_DIM), cosine, sine)
    v = dot(a_wide, w_value).astype(bf16).reshape(micro, rows, KV_HEADS, HEAD_DIM)
    q = q.astype(bf16).reshape(micro, rows, KV_HEADS, GROUP, HEAD_DIM)
    k = k.astype(bf16)
    s = jnp.einsum("bqhgd,bkhd->bhgqk", q, k, preferred_element_type=f32) * HEAD_DIM**-0.5
    s = jnp.where(allowed[:, None, None], s, masked_score)
    e = jnp.exp(s - jnp.max(s, axis=-1, keepdims=True))
    p = e / jnp.sum(e, axis=-1, keepdims=True)
    p_low = p.astype(bf16)
    o = jnp.einsum("bhgqk,bkhd->bqhgd", p_low, v, preferred_element_type=f32)
    o = o.reshape(micro * rows, QD).astype(bf16)
    m = h + dot(dot(o, spread).astype(bf16), w_output)
    n2, r2 = norm_parts(m)
    b = (n2 * ffn_gain).astype(bf16)
    b_wide = dot(b, spread).astype(bf16)
    gate = dot(b_wide, w_gate)
    up = dot(b_wide, w_up)
    hidden = (gate * jax.nn.sigmoid(gate) * up).astype(bf16)
    result = ((m + dot(hidden, w_down)) * live).astype(bf16)
    return result, (n1, r1, a, q, k, v, p, p_low, o, n2, r2, b, gate, up, hidden)


def backward(saved, upstream, weights, geo, spread):
    w_query, w_key, w_value, w_output, w_gate, w_up, w_down, attn_gain, ffn_gain = weights
    n1, r1, a, q, k, v, p, p_low, o, n2, r2, b, gate, up, hidden = saved
    live, cosine, sine, allowed = geo
    micro, rows = cosine.shape[:2]
    d3 = upstream.astype(f32) * live
    d3_low = d3.astype(bf16)
    dhidden = dot_t(d3_low, w_down)
    sig = jax.nn.sigmoid(gate)
    dg = (dhidden * up * sig * (1.0 + gate * (1.0 - sig))).astype(bf16)
    du = (dhidden * gate * sig).astype(bf16)
    db = gather_rows(dot_t(dg, w_gate) + dot_t(du, w_up), spread)
    dm = d3 + norm_back(db, n2, r2, ffn_gain)
    dffn = jnp.sum(db * n2, axis=0)
    dm_low = dm.astype(bf16)
    do = dot_t(dot_t(dm_low, w_output).astype(bf16), spread).astype(bf16)
    do = do.reshape(micro, rows, KV_HEADS, GROUP, HEAD_DIM)
    dp = jnp.einsum("bqhgd,bkhd->bhgqk", do, v, preferred_element_type=f32)
    dv = jnp.einsum("bhgqk,bqhgd->bkhd", p_low, do, preferred_element_type=f32)
    ds = (p * (dp - jnp.sum(p * dp, axis=-1, keepdims=True))).astype(bf16)
    dq = jnp.einsum("bhgqk,bkhd->bqhgd", ds, k, preferred_element_type=f32) * HEAD_DIM**-0.5
    dk = jnp.einsum("bhgqk,bqhgd->bkhd", ds, q, preferred_element_type=f32) * HEAD_DIM**-0.5
    dq = rotate(dq.reshape(micro, rows, HEADS, HEAD_DIM), cosine, -sine)
    dq = dq.reshape(micro * rows, QD).astype(bf16)
    dk = rotate(dk, cosine, -sine).reshape(micro * rows, KVD).astype(bf16)
    dv = dv.reshape(micro * rows, KVD).astype(bf16)
    da = gather_rows(dot_t(dq, w_query) + dot_t(dk, w_key) + dot_t(dv, w_value), spread)
    dh = dm + norm_back(da, n1, r1, attn_gain)
    dattn = jnp.sum(da * n1, axis=0)
    return dh.astype(bf16), (d3_low, dg, du, dm_low, dq, dk, dv, dattn, dffn)


def blocks(left_t, rows):
    return left_t.reshape((2,) * 6 + (rows, left_t.shape[-1]))


def pick(array, dim, index):
    return lax.index_in_dim(array, index, dim, keepdims=False)


def product(left_t, right):
    flat = left_t.reshape(-1, left_t.shape[-1])
    return dot(flat, right).reshape(left_t.shape[:-1] + (right.shape[-1],))


def first_halves(left_t, right, order, extra=None):
    dim = BITS.index(order[0])
    halves = []
    for index in (1, 0):
        value = product(pick(left_t, dim, index), right)
        if extra is not None:
            value = value + pick(extra, dim, index)
        halves.append(value.astype(bf16))
    return halves[1], halves[0]


def rotations(place, then):
    axes = "yzx"
    result = []
    for turn in range(3):
        turned = axes[turn:] + axes[:turn]
        result.append(tuple((axis, place) for axis in turned) + tuple((axis, then) for axis in turned))
    return result


ORDERS = (rotations(1, 0), rotations(0, 1))


def halving(kept, sent, order, left, last):
    bit = order[0]
    left = [other for other in left if other != bit]
    arrived = lax.ppermute(sent, "dp", partner_pairs(bit))
    if len(order) == 1:
        return (kept.astype(f32) + arrived.astype(f32)), None, left
    if last:
        return (kept.astype(f32) + arrived.astype(f32)).astype(bf16), None, left
    dim = left.index(order[1])
    next_sent = pick(kept, dim, 1).astype(f32) + pick(arrived, dim, 1).astype(f32)
    next_kept = pick(kept, dim, 0).astype(f32) + pick(arrived, dim, 0).astype(f32)
    return next_kept.astype(bf16), next_sent.astype(bf16), left


def reduce_three(members, orders):
    after = []
    for (left_t, right, extra), order in zip(members, orders):
        kept, sent = first_halves(left_t, right, order, extra)
        left = list(BITS)
        for step in range(3):
            kept, sent, left = halving(kept, sent, order[step:], left, step == 2)
        after.append(kept)
    return after, left


def finish(value, left, order):
    dim = left.index(order[0])
    kept, sent = pick(value, dim, 0), pick(value, dim, 1)
    for step in range(3):
        kept, sent, left = halving(kept, sent, order[step:], left, False)
    return kept


def xor_order(left_t):
    width = left_t.shape[-1]
    value = left_t.reshape(4, 4, 4, DOWN_ROWS, width)
    me = lax.axis_index("dp")
    for dim, shift in enumerate((4, 2, 0)):
        mine = gray((me >> shift) & 3)
        value = jnp.concatenate(
            [lax.dynamic_slice_in_dim(value, gray(mine ^ place), 1, dim) for place in range(4)],
            axis=dim,
        )
    return value


def body(
    inputs,
    starts,
    cotangent,
    w_query,
    w_key,
    w_value,
    w_output,
    w_gate,
    w_up,
    w_down,
    attn_gain,
    ffn_gain,
):
    section = lax.axis_index("section")
    micro, rows = starts.shape
    gains = jnp.concatenate([attn_gain, ffn_gain], axis=1)
    gain_row = jnp.pad(gains, ((0, 0), (0, D - gains.shape[1])))
    blank = jnp.zeros((1, D), bf16)
    slabs = (
        w_query[0],
        w_output[0],
        w_gate[0, :, :960],
        w_gate[0, :, 960:1920],
        w_up[0, :, :960],
        w_up[0, :, 960:1920],
        jnp.concatenate([w_gate[0, :, 1920:], w_key[0]], axis=1),
        jnp.concatenate([w_up[0, :, 1920:], w_value[0]], axis=1),
    )
    pieces = []
    for index, slab in enumerate(slabs):
        pieces += [slab, gain_row if index == 0 else blank]
    packed = jnp.concatenate(pieces + [w_down[0]], axis=0)[None]
    everything = lax.all_gather(packed, "dp", axis=0, tiled=True)

    def slab_of(index):
        part = everything[:, PADDED * index : PADDED * (index + 1)]
        return part.reshape(OWNERS * PADDED, D)

    mixed_gate, mixed_up = slab_of(6), slab_of(7)
    all_gains = everything[:, SLOT, : 2 * SLOT].astype(f32)
    weights = (
        slab_of(0),
        mixed_gate[:, 640:],
        mixed_up[:, 640:],
        slab_of(1),
        jnp.concatenate([slab_of(2), slab_of(3), mixed_gate[:, :640]], axis=1),
        jnp.concatenate([slab_of(4), slab_of(5), mixed_up[:, :640]], axis=1),
        everything[:, 8 * PADDED :].reshape(FF, D),
        all_gains[:, :SLOT].reshape(D),
        all_gains[:, SLOT:].reshape(D),
    )
    spread = spread_matrix()
    mine = own_spread()
    geo = geometry(starts)
    first_in = inputs.reshape(micro * rows, D)
    top = cotangent.reshape(micro * rows, D)

    made, _ = forward(first_in, weights, geo, spread)
    arrived = lax.ppermute(made, "section", [(0, 1)])
    source = jnp.where(section == 0, first_in, arrived)
    result, saved = forward(source, weights, geo, spread)
    back, _ = backward(saved, top, weights, geo, spread)
    returned = lax.ppermute(back, "section", [(1, 0)])
    upstream = jnp.where(section == 1, top, returned)
    grad_rows, grads = backward(saved, upstream, weights, geo, spread)
    d3_low, dg, du, dm_low, dq, dk, dv, dattn, dffn = grads
    a, o, b, hidden = saved[2], saved[8], saved[11], saved[14]

    a_t = blocks(dot_t(mine, a).astype(bf16), PADDED)
    o_t = blocks(dot_t(mine, o).astype(bf16), PADDED)
    b_t = blocks(dot_t(mine, b).astype(bf16), PADDED)
    hidden_t = blocks(xor_order(hidden.T), DOWN_ROWS)

    half = FF // 2
    outs = []
    for group, orders in enumerate(ORDERS):
        cut = slice(group * half, (group + 1) * half)
        down_cut = slice(0, 512) if group == 0 else slice(512, D)
        members = (
            (b_t, dg[:, cut], None),
            (b_t, du[:, cut], None),
            (hidden_t, d3_low[:, down_cut], None),
        )
        (gate_part, up_part, down_part), left = reduce_three(members, orders)
        pair = jnp.concatenate([gate_part, up_part], axis=-1)
        outs.append((finish(pair, left, orders[0][3:]), finish(down_part, left, orders[1][3:])))
    grad_gate = jnp.concatenate([outs[0][0][:SLOT, :half], outs[1][0][:SLOT, :half]], axis=1)
    grad_up = jnp.concatenate([outs[0][0][:SLOT, half:], outs[1][0][:SLOT, half:]], axis=1)
    grad_down = jnp.concatenate([outs[0][1], outs[1][1]], axis=1)

    owner = owner_of(jnp.arange(OWNERS, dtype=jnp.int32))
    choose = (owner[:, None] == jnp.arange(OWNERS, dtype=jnp.int32)[None, :]).astype(f32)
    both = jnp.concatenate([dattn.reshape(OWNERS, SLOT), dffn.reshape(OWNERS, SLOT)], axis=1)
    both = jnp.dot(choose, both, precision=lax.Precision.HIGHEST)
    extra = jnp.pad(both[:, None, :], ((0, 0), (SLOT, 0), (0, 512 - 2 * SLOT)))
    extra = extra.reshape((2,) * 6 + extra.shape[1:])
    dqkv = jnp.concatenate([dq, dk, dv], axis=1)
    cuts = (((0, 512), (512, 896), (0, 512)), ((896, 1280), (1280, 1600), (512, 960)))
    ends = []
    for group, orders in enumerate(ORDERS):
        (lo0, hi0), (lo1, hi1), (lo2, hi2) = cuts[group]
        members = (
            (a_t, dqkv[:, lo0:hi0], extra if group == 0 else None),
            (a_t, dqkv[:, lo1:hi1], None),
            (o_t, dm_low[:, lo2:hi2], None),
        )
        parts, left = reduce_three(members, orders)
        ends.append(finish(jnp.concatenate(parts, axis=-1), left, orders[2][3:]))
    dqkv_sum = jnp.concatenate([ends[0][:, :896], ends[1][:, :704]], axis=1)
    grad_output = jnp.concatenate([ends[0][:SLOT, 896:], ends[1][:SLOT, 704:]], axis=1)
    gain_sum = dqkv_sum[SLOT]
    return (
        result.reshape(1, micro, rows, D),
        grad_rows.reshape(1, micro, rows, D),
        dqkv_sum[None, :SLOT, :QD],
        dqkv_sum[None, :SLOT, QD : QD + KVD],
        dqkv_sum[None, :SLOT, QD + KVD :],
        grad_output[None],
        grad_gate[None],
        grad_up[None],
        grad_down[None],
        gain_sum[None, :SLOT],
        gain_sum[None, SLOT : 2 * SLOT],
    )


def solution(mesh):
    split = P("section", "dp", None)
    return jax.shard_map(
        body,
        mesh=mesh,
        in_specs=(P(None, "dp", None), P(None, "dp"), P(None, "dp", None))
        + (split,) * 7
        + (P("section", "dp"),) * 2,
        out_specs=(P("section", None, "dp", None),) * 2
        + (split,) * 7
        + (P("section", "dp"),) * 2,
        check_vma=False,
    )
```

```python
from functools import partial

import jax
import jax.numpy as jnp
from jax import lax
from jax.experimental import pallas as pl
from jax.experimental.pallas import tpu as pltpu
from jax.sharding import PartitionSpec as P

D = 960
HEADS = 15
KV_HEADS = 5
GROUP = HEADS // KV_HEADS
HEAD_DIM = 64
FF = 2560
QD = 960
KVD = 320
OWNERS = 64
SLOT = 15
PADDED = 16
DOWN_ROWS = 40

norm_eps = 1e-05
masked_score = -1e30
rope_base = 10000.0

f32 = jnp.float32
bf16 = jnp.bfloat16


def gray(value):
    return value ^ (value >> 1)


AXIS_SHIFT = {"y": 4, "z": 2, "x": 0}
BITS = (("y", 1), ("y", 0), ("z", 1), ("z", 0), ("x", 1), ("x", 0))


def partner_pairs(bit):
    axis, place = bit
    shift = AXIS_SHIFT[axis]
    pairs = []
    for source in range(OWNERS):
        coordinate = (source >> shift) & 3
        other = gray(gray(coordinate) ^ (1 << place))
        pairs.append((source, source + ((other - coordinate) << shift)))
    return pairs


def owner_of(position):
    me = lax.axis_index("dp")
    owner = 0
    for shift in (4, 2, 0):
        owner = owner + (gray(gray((me >> shift) & 3) ^ ((position >> shift) & 3)) << shift)
    return owner


def dot(left, right):
    return jnp.dot(left, right, preferred_element_type=f32)


def dot_t(left, right):
    return lax.dot_general(left, right, (((1,), (1,)), ((), ())), preferred_element_type=f32)


def spread_matrix():
    row = lax.broadcasted_iota(jnp.int32, (D, OWNERS * PADDED), 0)
    col = lax.broadcasted_iota(jnp.int32, (D, OWNERS * PADDED), 1)
    return ((row == SLOT * (col // PADDED) + col % PADDED) & (col % PADDED < SLOT)).astype(bf16)


def own_spread():
    row = lax.broadcasted_iota(jnp.int32, (OWNERS * PADDED, D), 0)
    col = lax.broadcasted_iota(jnp.int32, (OWNERS * PADDED, D), 1)
    owner = owner_of(row // PADDED)
    return ((col == SLOT * owner + row % PADDED) & (row % PADDED < SLOT)).astype(bf16)


CHUNK = 128
CHUNKS = 8
KV_CHUNKS = 3
PIECES = ((0, 960), (960, 1920), (1920, 2560))
SLABS = 8
VMEM_BYTES = 56 * 2**20


def mm(left, right):
    return lax.dot_general(left, right, (((1,), (0,)), ((), ())), preferred_element_type=f32)


def mm_t(left, right):
    return lax.dot_general(left, right, (((1,), (1,)), ((), ())), preferred_element_type=f32)


def mm_tl(left, right):
    return lax.dot_general(left, right, (((0,), (0,)), ((), ())), preferred_element_type=f32)


def lanes(shape):
    return lax.broadcasted_iota(jnp.int32, shape, len(shape) - 1)


def cut_chunk(value, index):
    width = value.shape[1]
    low = index * CHUNK
    high = min(low + CHUNK, width)
    part = value[:, low:high]
    if high - low < CHUNK:
        part = jnp.concatenate(
            [part, jnp.zeros((value.shape[0], CHUNK - (high - low)), value.dtype)], axis=1
        )
    return part


def turn(value, cosine, sine):
    first = lanes(value.shape) % HEAD_DIM < HEAD_DIM // 2
    swapped = jnp.where(
        first, pltpu.roll(value, CHUNK - HEAD_DIM // 2, 1), pltpu.roll(value, HEAD_DIM // 2, 1)
    )
    return value * cosine + swapped * sine


def doubled(chunk, half):
    other = pltpu.roll(chunk, HEAD_DIM, 1)
    low = lanes(chunk.shape) < HEAD_DIM
    return jnp.where(low, chunk, other) if half == 0 else jnp.where(low, other, chunk)


def only(chunk, half):
    keep = (lanes(chunk.shape) < HEAD_DIM) == (half == 0)
    return jnp.where(keep, chunk, jnp.zeros_like(chunk))


def load_weights(big_ref, down_ref, slabs, down, sems, order):
    copies = {}
    for index in order:
        if index < SLABS:
            copies[index] = pltpu.make_async_copy(
                big_ref.at[:, pl.ds(PADDED * index, PADDED), :], slabs.at[index], sems.at[index]
            )
        else:
            copies[index] = pltpu.make_async_copy(down_ref, down, sems.at[index])
        copies[index].start()
    return copies


def slab(slabs, index, low=0, high=D):
    return slabs[index].reshape(OWNERS * PADDED, D)[:, low:high]


def gate_slab(slabs, piece):
    return slab(slabs, 2 + piece) if piece < 2 else slab(slabs, 6, 0, 640)


def up_slab(slabs, piece):
    return slab(slabs, 4 + piece) if piece < 2 else slab(slabs, 7, 0, 640)


def unit_rows(value):
    inverse = lax.rsqrt(jnp.mean(value * value, axis=-1, keepdims=True) + norm_eps)
    return value * inverse, inverse


def forward_kernel(
    x_ref, cos_ref, sin_ref, allow_ref, live_ref, gains_ref, spread_ref, big_ref, down_ref,
    y_ref, q_ref, k_ref, v_ref, p_ref, o_ref, m_ref, g0_ref, g1_ref, g2_ref, u0_ref, u1_ref, u2_ref,
    slabs, down, sems,
):
    copies = load_weights(big_ref, down_ref, slabs, down, sems, (0, 6, 7, 1, 2, 4, 3, 5, 8))
    cosine, sine = cos_ref[...], sin_ref[...]
    allowed = allow_ref[...] > 0
    spread = spread_ref[...]
    h = x_ref[...].astype(f32)
    n1, _ = unit_rows(h)
    a = (n1 * gains_ref[0:1, :]).astype(bf16)
    a_wide = mm(a, spread).astype(bf16)
    copies[0].wait()
    q_all = mm(a_wide, slab(slabs, 0))
    copies[6].wait()
    k_all = mm(a_wide, slab(slabs, 6, 640, 960))
    copies[7].wait()
    v_all = mm(a_wide, slab(slabs, 7, 640, 960))
    keys, values = [], []
    for index in range(KV_CHUNKS):
        k_chunk = turn(cut_chunk(k_all, index), cosine, sine)
        v_chunk = cut_chunk(v_all, index)
        k_ref[index] = k_chunk.astype(bf16)
        v_ref[index] = v_chunk.astype(bf16)
        for half in range(2):
            keys.append(doubled(k_chunk, half).astype(bf16))
            values.append(doubled(v_chunk, half).astype(bf16))
    mixed = []
    for index in range(CHUNKS):
        q_chunk = turn(cut_chunk(q_all, index), cosine, sine).astype(bf16)
        q_ref[index] = q_chunk
        total = None
        for half in range(2):
            head = 2 * index + half
            if head >= HEADS:
                continue
            s = mm_t(only(q_chunk, half), keys[head // GROUP]) * HEAD_DIM**-0.5
            s = jnp.where(allowed, s, masked_score)
            e = jnp.exp(s - jnp.max(s, axis=-1, keepdims=True))
            p = e / jnp.sum(e, axis=-1, keepdims=True)
            p_ref[head] = p
            part = mm(p.astype(bf16), only(values[head // GROUP], half))
            total = part if total is None else total + part
        mixed.append(total)
    o = jnp.concatenate(mixed, axis=1)[:, :QD].astype(bf16)
    o_ref[...] = o
    o_wide = mm(o, spread).astype(bf16)
    copies[1].wait()
    m = h + mm(o_wide, slab(slabs, 1))
    m_ref[...] = m
    n2, _ = unit_rows(m)
    b = (n2 * gains_ref[1:2, :]).astype(bf16)
    b_wide = mm(b, spread).astype(bf16)
    hiddens = []
    for piece, (g_ref, u_ref) in enumerate(((g0_ref, u0_ref), (g1_ref, u1_ref), (g2_ref, u2_ref))):
        if piece < 2:
            copies[2 + piece].wait()
            copies[4 + piece].wait()
        gate = mm(b_wide, gate_slab(slabs, piece))
        up = mm(b_wide, up_slab(slabs, piece))
        g_ref[...] = gate
        u_ref[...] = up
        hiddens.append((gate * lax.logistic(gate) * up).astype(bf16))
    copies[8].wait()
    total = m
    for (low, high), hidden in zip(PIECES, hiddens):
        total = total + mm(hidden, down[low:high, :])
    y_ref[...] = (total * live_ref[...]).astype(bf16)


def narrow(value, spread):
    high = value.astype(bf16)
    low = (value - high.astype(f32)).astype(bf16)
    return mm_t(high, spread) + mm_t(low, spread)


def norm_grad(grad, normal, inverse, gain):
    scaled = grad * gain
    inner = jnp.mean(scaled * normal, axis=-1, keepdims=True)
    return inverse * (scaled - normal * inner)


def feed_forward_back_kernel(
    top_ref, m_ref, g0_ref, g1_ref, g2_ref, u0_ref, u1_ref, u2_ref,
    live_ref, gains_ref, spread_ref, big_ref, down_ref,
    dm_ref, low_ref, d3_ref, dg0_ref, dg1_ref, dg2_ref, du0_ref, du1_ref, du2_ref,
    dgain_ref, b_ref, h0_ref, h1_ref, h2_ref,
    slabs, down, sems,
):
    copies = load_weights(big_ref, down_ref, slabs, down, sems, (8, 2, 4, 3, 5, 6, 7))
    spread = spread_ref[...]
    gain_f = gains_ref[1:2, :]
    d3 = top_ref[...].astype(f32) * live_ref[...]
    d3_low = d3.astype(bf16)
    d3_ref[...] = d3_low
    n2, r2 = unit_rows(m_ref[...])
    b_ref[...] = (n2 * gain_f).astype(bf16)
    copies[8].wait()
    wide = jnp.zeros((d3.shape[0], OWNERS * PADDED), f32)
    refs = (
        (g0_ref, u0_ref, dg0_ref, du0_ref, h0_ref),
        (g1_ref, u1_ref, dg1_ref, du1_ref, h1_ref),
        (g2_ref, u2_ref, dg2_ref, du2_ref, h2_ref),
    )
    for piece, (g_ref, u_ref, dg_ref, du_ref, hid_ref) in enumerate(refs):
        low, high = PIECES[piece]
        dhidden = mm_t(d3_low, down[low:high, :])
        gate, up = g_ref[...], u_ref[...]
        sig = lax.logistic(gate)
        act = gate * sig
        hid_ref[...] = (act * up).astype(bf16)
        dg = (dhidden * up * sig * (1.0 + gate * (1.0 - sig))).astype(bf16)
        du = (dhidden * act).astype(bf16)
        dg_ref[...] = dg
        du_ref[...] = du
        if piece < 2:
            copies[2 + piece].wait()
            copies[4 + piece].wait()
        else:
            copies[6].wait()
            copies[7].wait()
        wide = wide + mm_t(dg, gate_slab(slabs, piece)) + mm_t(du, up_slab(slabs, piece))
    db = narrow(wide, spread)
    dgain_ref[...] = jnp.sum(db * n2, axis=0, keepdims=True)
    dm = d3 + norm_grad(db, n2, r2, gain_f)
    dm_ref[...] = dm
    low_ref[...] = dm.astype(bf16)


def attention_back_kernel(
    x_ref, dm_ref, low_ref, q_ref, k_ref, v_ref, p_ref,
    cos_ref, sin_ref, gains_ref, spread_ref, big_ref,
    dh_ref, dq_ref, dk_ref, dv_ref, dgain_ref, a_ref,
    slabs, sems,
):
    copies = load_weights(big_ref, None, slabs, None, sems, (1, 0, 6, 7))
    cosine, sine = cos_ref[...], sin_ref[...]
    spread = spread_ref[...]
    gain_a = gains_ref[0:1, :]
    copies[1].wait()
    do = mm_t(mm_t(low_ref[...], slab(slabs, 1)).astype(bf16), spread).astype(bf16)
    keys, values = [], []
    for index in range(KV_CHUNKS):
        k_chunk, v_chunk = k_ref[index].astype(f32), v_ref[index].astype(f32)
        for half in range(2):
            keys.append(doubled(k_chunk, half).astype(bf16))
            values.append(doubled(v_chunk, half).astype(bf16))
    dk_sums, dv_sums = [None] * KV_HEADS, [None] * KV_HEADS
    dq_parts = []
    for index in range(CHUNKS):
        do_chunk = cut_chunk(do, index)
        q_chunk = q_ref[index]
        total = None
        for half in range(2):
            head = 2 * index + half
            if head >= HEADS:
                continue
            group = head // GROUP
            do_head, q_head = only(do_chunk, half), only(q_chunk, half)
            p = p_ref[head]
            dp = mm_t(do_head, values[group])
            dv = mm_tl(p.astype(bf16), do_head)
            ds = (p * (dp - jnp.sum(p * dp, axis=-1, keepdims=True))).astype(bf16)
            dk = mm_tl(ds, q_head)
            part = mm(ds, only(keys[group], half))
            total = part if total is None else total + part
            dk_sums[group] = dk if dk_sums[group] is None else dk_sums[group] + dk
            dv_sums[group] = dv if dv_sums[group] is None else dv_sums[group] + dv
        dq_parts.append(turn(total * HEAD_DIM**-0.5, cosine, -sine))
    dq = jnp.concatenate(dq_parts, axis=1)[:, :QD].astype(bf16)
    low_lanes = lanes((do.shape[0], CHUNK)) < HEAD_DIM
    dk_parts, dv_parts = [], []
    for index in range(KV_CHUNKS):
        both = []
        for sums in (dk_sums, dv_sums):
            halves = []
            for half in range(2):
                group = 2 * index + half
                if group < KV_HEADS:
                    halves.append(sums[group] + pltpu.roll(sums[group], HEAD_DIM, 1))
                else:
                    halves.append(jnp.zeros_like(sums[0]))
            both.append(jnp.where(low_lanes, halves[0], halves[1]))
        dk_parts.append(turn(both[0] * HEAD_DIM**-0.5, cosine, -sine))
        dv_parts.append(both[1])
    dk = jnp.concatenate(dk_parts, axis=1)[:, :KVD].astype(bf16)
    dv = jnp.concatenate(dv_parts, axis=1)[:, :KVD].astype(bf16)
    dq_ref[...] = dq
    dk_ref[...] = dk
    dv_ref[...] = dv
    h = x_ref[...].astype(f32)
    n1, r1 = unit_rows(h)
    a_ref[...] = (n1 * gain_a).astype(bf16)
    copies[0].wait()
    copies[6].wait()
    copies[7].wait()
    wide = (
        mm_t(dq, slab(slabs, 0))
        + mm_t(dk, slab(slabs, 6, 640, 960))
        + mm_t(dv, slab(slabs, 7, 640, 960))
    )
    da = narrow(wide, spread)
    dgain_ref[...] = jnp.sum(da * n1, axis=0, keepdims=True)
    dh = dm_ref[...] + norm_grad(da, n1, r1, gain_a)
    dh_ref[...] = dh.astype(bf16)


def takes(microseconds):
    return pl.CostEstimate(
        flops=int(microseconds * 1.1e9), bytes_accessed=int(microseconds * 1e6), transcendentals=0
    )


def specs(count, anywhere=0):
    return [pl.BlockSpec(memory_space=pltpu.VMEM)] * count + [
        pl.BlockSpec(memory_space=pl.ANY)
    ] * anywhere


def weight_scratch():
    return [
        pltpu.VMEM((SLABS, OWNERS, PADDED, D), bf16),
        pltpu.VMEM((FF, D), bf16),
        pltpu.SemaphoreType.DMA((SLABS + 1,)),
    ]


def shapes(entries):
    return [jax.ShapeDtypeStruct(shape, kind) for shape, kind in entries]


def forward(x, tables, gains, spread, big, down):
    cosine, sine, allowed, live = tables
    rows = x.shape[0]
    widths = [high - low for low, high in PIECES]
    out = shapes(
        [
            ((rows, D), bf16),
            ((CHUNKS, rows, CHUNK), bf16),
            ((KV_CHUNKS, rows, CHUNK), bf16),
            ((KV_CHUNKS, rows, CHUNK), bf16),
            ((HEADS, rows, rows), f32),
            ((rows, QD), bf16),
            ((rows, D), f32),
        ]
        + [((rows, width), f32) for width in widths * 2]
    )
    return pl.pallas_call(
        forward_kernel,
        out_shape=out,
        in_specs=specs(7, 2),
        out_specs=specs(len(out)),
        scratch_shapes=weight_scratch(),
        compiler_params=pltpu.CompilerParams(vmem_limit_bytes=VMEM_BYTES),
        name="layer_forward",
        cost_estimate=takes(13),
    )(x, cosine, sine, allowed, live, gains, spread, big, down)


def feed_forward_back(top, saved, tables, gains, spread, big, down):
    live = tables[3]
    rows = top.shape[0]
    widths = [high - low for low, high in PIECES]
    out = shapes(
        [((rows, D), f32), ((rows, D), bf16), ((rows, D), bf16)]
        + [((rows, width), bf16) for width in widths * 2]
        + [((1, D), f32), ((rows, D), bf16)]
        + [((rows, width), bf16) for width in widths]
    )
    return pl.pallas_call(
        feed_forward_back_kernel,
        out_shape=out,
        in_specs=specs(11, 2),
        out_specs=specs(len(out)),
        scratch_shapes=weight_scratch(),
        compiler_params=pltpu.CompilerParams(vmem_limit_bytes=VMEM_BYTES),
        name="feed_forward_back",
        cost_estimate=takes(14),
    )(top, *saved[5:], live, gains, spread, big, down)


def attention_back(x, dm, dm_low, saved, tables, gains, spread, big):
    cosine, sine, _, _ = tables
    rows = x.shape[0]
    out = shapes(
        [((rows, D), bf16), ((rows, QD), bf16), ((rows, KVD), bf16), ((rows, KVD), bf16)]
        + [((1, D), f32), ((rows, D), bf16)]
    )
    scratch = weight_scratch()
    return pl.pallas_call(
        attention_back_kernel,
        out_shape=out,
        in_specs=specs(11, 1),
        out_specs=specs(len(out)),
        scratch_shapes=[scratch[0], scratch[2]],
        compiler_params=pltpu.CompilerParams(vmem_limit_bytes=VMEM_BYTES),
        name="attention_back",
        cost_estimate=takes(11.5),
    )(x, dm, dm_low, *saved[:4], cosine, sine, gains, spread, big)


def tables_of(starts):
    micro, rows = starts.shape
    local = jnp.arange(rows, dtype=jnp.int32)
    live = (starts <= local).reshape(-1)
    position = jnp.where(starts <= local, local - starts, 0).astype(f32).reshape(-1, 1)
    lane = jnp.arange(CHUNK, dtype=jnp.int32)
    turn_index = (lane % (HEAD_DIM // 2)).astype(f32)
    angles = position * rope_base ** (-2.0 * turn_index / HEAD_DIM)
    sign = jnp.where(lane % HEAD_DIM < HEAD_DIM // 2, -1.0, 1.0).astype(f32)
    row = jnp.arange(micro * rows, dtype=jnp.int32)
    begin = starts.reshape(-1, 1)
    column = row[None, :]
    same = (row[:, None] // rows) == (column // rows)
    inside = (column % rows >= begin) & (column <= row[:, None])
    allowed = (same & inside) | (row[:, None] == column)
    return jnp.cos(angles), jnp.sin(angles) * sign, allowed.astype(f32), live.astype(f32)[:, None]


STREAM_KINDS = (("a", "gain"), ("b",), ("b",), ("h0", "h1"), ("o", "h2"))
STREAM_RIGHTS = (14, 20, 20, 8, 16)
STREAM_CHUNKS = (14, 20, 20, 16, 12)
LEFT_ROWS = OWNERS // 2 * PADDED


def rotations(place, then):
    axes = "yzx"
    result = []
    for turned in (axes[start:] + axes[:start] for start in range(3)):
        result.append(
            tuple((axis, place) for axis in turned) + tuple((axis, then) for axis in turned)
        )
    return result


HIGH_FIRST, LOW_FIRST = rotations(1, 0), rotations(0, 1)
ORDERS = (HIGH_FIRST[0], LOW_FIRST[0], LOW_FIRST[1], HIGH_FIRST[1], HIGH_FIRST[2])
GROUPS = ((0, 3, 4), (1, 2))


def split_bit(value, dim, bits):
    shape = value.shape[1:]
    view = value.reshape((2**dim, 2, 2 ** (bits - 1 - dim)) + shape)
    return [view[:, index].reshape((2 ** (bits - 1),) + shape) for index in (0, 1)]


def chunks_of(value):
    count = (value.shape[1] + CHUNK - 1) // CHUNK
    return [cut_chunk(value, index) for index in range(count)]


def write_stream(stream, lefts, rights, keep_ref, pack_ref):
    rows = rights[0].shape[0]
    dim = BITS.index(ORDERS[stream][0])
    base = 0
    for index, left in enumerate(lefts):
        kept, sent = split_bit(left, dim, 6)
        keep_ref[index] = kept
        pack_ref[base : base + LEFT_ROWS, :] = sent.reshape(LEFT_ROWS, rows)
        base += LEFT_ROWS
    for chunk in rights:
        pack_ref[base : base + rows, :] = chunk
        base += rows


def in_order(mine, value):
    return mm_t(mine, value).astype(bf16).reshape(OWNERS, PADDED, value.shape[0])


def late_operand_kernel(
    mine_ref, a_ref, attn_ref, ffn_ref, dq_ref, dk_ref, dv_ref, keep_ref, pack_ref
):
    mine = mine_ref[...]
    rows = a_ref.shape[0]
    gain = jnp.concatenate([attn_ref[...], ffn_ref[...], jnp.zeros((rows - 2, D), f32)], axis=0)
    lefts = in_order(mine, a_ref[...]), in_order(mine, gain.astype(bf16))
    dq, dk, dv = dq_ref[...], dk_ref[...], dv_ref[...]
    tail = jnp.concatenate([dq[:, 896:], dk[:, 256:]], axis=1)
    identity = lax.broadcasted_iota(jnp.int32, (rows, CHUNK), 0) == lanes((rows, CHUNK))
    rights = chunks_of(dq)[:7] + chunks_of(dk)[:2] + [tail] + chunks_of(dv)
    write_stream(0, lefts, rights + [identity.astype(f32).astype(bf16)], keep_ref, pack_ref)


def early_operand_kernel(
    owner_ref, mine_ref, b_ref, o_ref, h0_ref, h1_ref, h2_ref, dm_ref, d3_ref,
    dg0_ref, dg1_ref, dg2_ref, du0_ref, du1_ref, du2_ref,
    *rest,
):
    keeps, packs = rest[:4], rest[4:8]
    turned, lefts = rest[8:]
    mine = mine_ref[...]
    rows = b_ref.shape[0]

    hidden = jnp.concatenate([h0_ref[...], h1_ref[...], h2_ref[...]], axis=1).astype(f32)
    turned[...] = hidden.T.reshape(OWNERS, DOWN_ROWS, rows)

    @pl.loop(0, OWNERS)
    def _(place):
        block = turned[owner_ref[place]]
        lefts[0, place] = block[0:16].astype(bf16)
        lefts[1, place] = block[16:32].astype(bf16)
        lefts[2, place] = jnp.concatenate(
            [block[32:40], jnp.zeros((8, rows), f32)], axis=0
        ).astype(bf16)

    b = in_order(mine, b_ref[...])
    o = in_order(mine, o_ref[...])
    dg = jnp.concatenate([dg0_ref[...], dg1_ref[...], dg2_ref[...]], axis=1)
    du = jnp.concatenate([du0_ref[...], du1_ref[...], du2_ref[...]], axis=1)
    d3, dm = chunks_of(d3_ref[...]), chunks_of(dm_ref[...])
    write_stream(1, (b,), chunks_of(dg), keeps[0], packs[0])
    write_stream(2, (b,), chunks_of(du), keeps[1], packs[1])
    write_stream(3, (lefts[0], lefts[1]), d3, keeps[2], packs[2])
    write_stream(4, (o, lefts[2]), dm + d3, keeps[3], packs[3])


def operand_shapes(streams, rows):
    return shapes(
        [((len(STREAM_KINDS[s]), OWNERS // 2, PADDED, rows), bf16) for s in streams]
        + [
            ((len(STREAM_KINDS[s]) * LEFT_ROWS + STREAM_RIGHTS[s] * rows, CHUNK), bf16)
            for s in streams
        ]
    )


def early_operands(mine, b, o, hidden, dm_low, d3, dg, du):
    rows = b.shape[0]
    out = operand_shapes((1, 2, 3, 4), rows)
    owners = owner_of(jnp.arange(OWNERS, dtype=jnp.int32))
    result = pl.pallas_call(
        early_operand_kernel,
        out_shape=out,
        in_specs=[pl.BlockSpec(memory_space=pltpu.SMEM)] + specs(14),
        out_specs=specs(len(out)),
        scratch_shapes=[
            pltpu.VMEM((OWNERS, DOWN_ROWS, rows), f32),
            pltpu.VMEM((3, OWNERS, PADDED, rows), bf16),
        ],
        compiler_params=pltpu.CompilerParams(vmem_limit_bytes=VMEM_BYTES),
        name="early_operands",
        cost_estimate=takes(7),
    )(owners, mine, b, o, *hidden, dm_low, d3, *dg, *du)
    return result[:4], result[4:]


def late_operands(mine, a, dattn, dffn, dq, dk, dv):
    out = operand_shapes((0,), a.shape[0])
    return pl.pallas_call(
        late_operand_kernel,
        out_shape=out,
        in_specs=specs(7),
        out_specs=specs(2),
        compiler_params=pltpu.CompilerParams(vmem_limit_bytes=VMEM_BYTES),
        name="late_operands",
        cost_estimate=takes(4),
    )(mine, a, dattn, dffn, dq, dk, dv)


def product_kernel(streams, *refs):
    count = len(streams)
    keeps, packs, others = (
        dict(zip(streams, refs[count * part : count * (part + 1)])) for part in range(3)
    )
    outs = {s: refs[3 * count + 2 * i : 3 * count + 2 * i + 2] for i, s in enumerate(streams)}
    step = pl.program_id(0)

    def left_of(stream, kind):
        kept = keeps[stream][kind].reshape(LEFT_ROWS, CHUNK)
        window = pl.ds(kind * LEFT_ROWS, LEFT_ROWS)
        return jnp.concatenate([kept, others[stream][window, :]], axis=1)

    def right_of(stream, chunk):
        start = len(STREAM_KINDS[stream]) * LEFT_ROWS + chunk * CHUNK
        if not isinstance(start, int):
            start = pl.multiple_of(start, CHUNK)
        window = pl.ds(start, CHUNK)
        return jnp.concatenate([packs[stream][window, :], others[stream][window, :]], axis=0)

    def right_pair(stream, first, second):
        return jnp.concatenate([right_of(stream, first), right_of(stream, second)], axis=1)

    def blocks_of(value):
        return value.reshape(OWNERS // 2, PADDED, CHUNK)

    def store(stream, place, value):
        dim = [bit for bit in BITS if bit != ORDERS[stream][0]].index(ORDERS[stream][1])
        kept, sent = split_bit(value.astype(bf16), dim, 5)
        outs[stream][0][place] = kept
        outs[stream][1][place] = sent

    def usual(stream, kind, first):
        value = mm(left_of(stream, kind), right_pair(stream, first, first + 1))
        store(stream, 0, blocks_of(value[:, :CHUNK]))
        store(stream, 1, blocks_of(value[:, CHUNK:]))

    def short_rows(stream, kind, first):
        value = mm(left_of(stream, kind), right_pair(stream, first, first + 4))
        parts = [blocks_of(part)[:, :8] for part in (value[:, :CHUNK], value[:, CHUNK:])]
        return jnp.concatenate(parts, axis=1)

    def when(condition, action):
        pl.when(condition)(action)

    if 0 in streams:
        when(step < 6, lambda: usual(0, 0, 2 * step))

        @pl.when(step == 6)
        def _():
            store(0, 0, blocks_of(mm(left_of(0, 0), right_of(0, 12))))
            store(0, 1, blocks_of(mm(left_of(0, 1), right_of(0, 13))))

    if 1 in streams:
        usual(1, 0, 2 * step)
    if 2 in streams:
        usual(2, 0, 2 * step)
    if 3 in streams:
        when(step < 4, lambda: usual(3, 0, 2 * step))
        when(step >= 4, lambda: usual(3, 1, 2 * step - 8))
    if 4 in streams:
        when(step < 4, lambda: usual(4, 0, 2 * step))

        @pl.when((step >= 4) & (step < 6))
        def _():
            for place in range(2):
                store(4, place, short_rows(4, 1, 8 + 2 * (step - 4) + place))


def products(streams, keeps, packs, others):
    out, out_specs = [], []
    for stream in streams:
        last = STREAM_CHUNKS[stream] // 2 - 1
        for _ in range(2):
            out.append(((STREAM_CHUNKS[stream], OWNERS // 4, PADDED, CHUNK), bf16))
            out_specs.append(
                pl.BlockSpec(
                    (2, OWNERS // 4, PADDED, CHUNK),
                    lambda step, last=last: (jnp.minimum(step, last), 0, 0, 0),
                )
            )
    result = pl.pallas_call(
        partial(product_kernel, streams),
        grid=(max(STREAM_CHUNKS[stream] for stream in streams) // 2,),
        out_shape=shapes(out),
        in_specs=specs(3 * len(streams)),
        out_specs=out_specs,
        compiler_params=pltpu.CompilerParams(vmem_limit_bytes=VMEM_BYTES),
        name="grad_products",
        cost_estimate=takes(sum(STREAM_CHUNKS[stream] for stream in streams) * 0.2),
    )(*keeps, *packs, *others)
    return list(result[0::2]), list(result[1::2])


def together(values):
    return list(lax.optimization_barrier(tuple(values)))


def send(values, bits):
    return together([lax.ppermute(v, "dp", partner_pairs(b)) for v, b in zip(values, bits)])


def halved(kept, arrived, dim):
    size = kept.shape[1]
    view = (kept.shape[0], 2**dim, 2, size >> (dim + 1)) + kept.shape[2:]
    flat = (kept.shape[0], size // 2) + kept.shape[2:]
    first, second = kept.reshape(view), arrived.reshape(view)
    return tuple(
        (first[:, :, index].astype(f32) + second[:, :, index].astype(f32))
        .astype(bf16)
        .reshape(flat)
        for index in (0, 1)
    )


def exchanged(streams, packs):
    return send(packs, [ORDERS[stream][0] for stream in streams])


def three_steps(streams, keeps, packs, others):
    orders = [ORDERS[stream] for stream in streams]
    kept, sent = products(streams, keeps, packs, others)
    arrived = send(sent, [order[1] for order in orders])
    for index, order in enumerate(orders):
        left = [bit for bit in BITS if bit not in order[:2]]
        kept[index], sent[index] = halved(kept[index], arrived[index], left.index(order[2]))
    return kept, send(sent, [order[2] for order in orders])


def last_steps(parts):
    kept, sent, rest = [], [], []
    for members, (keeps, arrived) in zip(GROUPS, parts):
        order = ORDERS[members[0]]
        left = [bit for bit in BITS if bit not in order[:3]]
        halves = [halved(k, a, left.index(order[3])) for k, a in zip(keeps, arrived)]
        kept.append(jnp.concatenate([half[0] for half in halves], axis=0))
        sent.append(jnp.concatenate([half[1] for half in halves], axis=0))
        rest.append((left, order[3:]))
    for step in range(3):
        arrived = send(sent, [order[step] for _, order in rest])
        for group, (left, order) in enumerate(rest):
            left.remove(order[step])
            if step < 2:
                dim = left.index(order[step + 1])
                kept[group], sent[group] = halved(kept[group], arrived[group], dim)
    return kept, arrived


def result_kernel(
    kept0_ref, kept1_ref, came0_ref, came1_ref,
    query_ref, key_ref, value_ref, output_ref, gate_ref, up_ref, down_ref, attn_ref, ffn_ref,
):
    def block(group, index):
        kept, came = ((kept0_ref, came0_ref), (kept1_ref, came1_ref))[group]
        return kept[index, 0].astype(f32) + came[index, 0].astype(f32)

    def put(ref, low, high, value, column):
        width = min(CHUNK, ref.shape[-1] - column)
        value = value[: high - low, :width]
        if len(ref.shape) == 3:
            ref[low:high, 0, column : column + width] = value
        else:
            ref[low:high, column : column + width] = value

    half = HEAD_DIM
    for index in range(7):
        put(query_ref, 0, SLOT, block(0, index), CHUNK * index)
    for index in range(2):
        put(key_ref, 0, SLOT, block(0, 7 + index), CHUNK * index)
    tail = block(0, 9)
    put(query_ref, 0, SLOT, tail, 896)
    put(key_ref, 0, SLOT, tail[:, half:], 256)
    for index in range(3):
        put(value_ref, 0, SLOT, block(0, 10 + index), CHUNK * index)
    gains = block(0, 13)
    eye = (lax.broadcasted_iota(jnp.int32, (8, CHUNK), 0) == lanes((8, CHUNK))).astype(f32)
    turned = lax.dot_general(
        eye, gains, (((1,), (1,)), ((), ())),
        preferred_element_type=f32, precision=lax.Precision.HIGHEST,
    )
    attn_ref[...] = turned[0:1, :SLOT]
    ffn_ref[...] = turned[1:2, :SLOT]
    for index in range(8):
        put(down_ref, 0, 16, block(0, 14 + index), CHUNK * index)
        put(down_ref, 16, 32, block(0, 22 + index), CHUNK * index)
        put(output_ref, 0, SLOT, block(0, 30 + index), CHUNK * index)
    for index in range(4):
        both = block(0, 38 + index)
        put(down_ref, 32, 40, both[:8], CHUNK * index)
        put(down_ref, 32, 40, both[8:], CHUNK * (index + 4))
    for index in range(20):
        put(gate_ref, 0, SLOT, block(1, index), CHUNK * index)
        put(up_ref, 0, SLOT, block(1, 20 + index), CHUNK * index)


def weight_results(kept, came):
    wide = [(SLOT, 1, width) for width in (QD, KVD, KVD, D, FF, FF)]
    out = shapes([(shape, f32) for shape in wide + [(DOWN_ROWS, D), (1, SLOT), (1, SLOT)]])
    result = pl.pallas_call(
        result_kernel,
        out_shape=out,
        in_specs=specs(4),
        out_specs=specs(len(out)),
        name="weight_results",
        cost_estimate=takes(3),
    )(*kept, *came)
    slots = tuple(value.transpose(1, 0, 2) for value in result[:6])
    return slots + (result[6][None],) + tuple(result[7:])


def pack_kernel(q_ref, k_ref, v_ref, o_ref, g_ref, u_ref, d_ref, gain_ref, out_ref):
    blank = jnp.zeros((PADDED - SLOT, D), bf16)
    g, u = g_ref[0], u_ref[0]
    plain = (
        q_ref[0],
        o_ref[0],
        g[:, :960],
        g[:, 960:1920],
        u[:, :960],
        u[:, 960:1920],
        jnp.concatenate([g[:, 1920:], k_ref[0]], axis=1),
        jnp.concatenate([u[:, 1920:], v_ref[0]], axis=1),
    )
    for index, value in enumerate(plain):
        last = gain_ref[...] if index == 0 else blank
        full = jnp.concatenate([value.astype(f32), last.astype(f32)], axis=0)
        out_ref[0, PADDED * index : PADDED * (index + 1), :] = full.astype(bf16)
    out_ref[0, PADDED * SLABS :, :] = d_ref[0]


def packed_weights(w_query, w_key, w_value, w_output, w_gate, w_up, w_down, attn_gain, ffn_gain):
    gains = jnp.concatenate([attn_gain, ffn_gain], axis=1)
    gain_row = jnp.pad(gains, ((0, 0), (0, D - gains.shape[1])))
    return pl.pallas_call(
        pack_kernel,
        out_shape=jax.ShapeDtypeStruct((1, PADDED * SLABS + DOWN_ROWS, D), bf16),
        in_specs=specs(8),
        out_specs=pl.BlockSpec(memory_space=pltpu.VMEM),
        name="pack_weights",
        cost_estimate=takes(2),
    )(w_query, w_key, w_value, w_output, w_gate, w_up, w_down, gain_row)


def body(inputs, starts, cotangent, *weights):
    section = lax.axis_index("section")
    micro, rows = starts.shape
    everything = lax.all_gather(packed_weights(*weights), "dp", axis=0, tiled=True)
    down = everything[:, SLABS * PADDED :].reshape(FF, D)
    all_gains = everything[:, SLOT, : 2 * SLOT].astype(f32)
    all_gains = jnp.stack([all_gains[:, :SLOT].reshape(D), all_gains[:, SLOT:].reshape(D)])
    spread = spread_matrix()
    mine = own_spread()
    tables = tables_of(starts)
    first_in = inputs.reshape(micro * rows, D)
    top = cotangent.reshape(micro * rows, D)
    shared = (tables, all_gains, spread, everything)

    made = forward(first_in, *shared, down)[0]
    arrived = lax.ppermute(made, "section", [(0, 1)])
    source = jnp.where(section == 0, first_in, arrived)
    result, *saved = forward(source, *shared, down)

    dm, dm_low = feed_forward_back(top, saved, *shared, down)[:2]
    back = attention_back(source, dm, dm_low, saved, *shared)[0]
    returned = lax.ppermute(back, "section", [(1, 0)])
    upstream = jnp.where(section == 1, top, returned)

    ffn = feed_forward_back(upstream, saved, *shared, down)
    dm, dm_low, d3, dffn, b, hidden = ffn[0], ffn[1], ffn[2], ffn[9], ffn[10], ffn[11:14]
    keeps, packs = early_operands(mine, b, saved[4], hidden, dm_low, d3, ffn[3:6], ffn[6:9])
    dm, dm_low, *packs = together([dm, dm_low, *packs])
    others = exchanged((1, 2, 3, 4), packs)
    grad_rows, dq, dk, dv, dattn, a = attention_back(source, dm, dm_low, saved, *shared)
    a, *others = together([a, *others])
    late_keep, late_pack = late_operands(mine, a, dattn, dffn, dq, dk, dv)
    last = exchanged((0,), [late_pack])

    gate_up = three_steps((1, 2), keeps[:2], packs[:2], others[:2])
    down_out = three_steps((3, 4), keeps[2:], packs[2:], others[2:])
    query = three_steps((0,), [late_keep], [late_pack], last)
    first_group = (query[0] + down_out[0], query[1] + down_out[1])
    sums = weight_results(*last_steps((first_group, gate_up)))
    rows_out = (result.reshape(1, micro, rows, D), grad_rows.reshape(1, micro, rows, D))
    return rows_out + sums


def solution(mesh):
    split = P("section", "dp", None)
    return jax.shard_map(
        body,
        mesh=mesh,
        in_specs=(P(None, "dp", None), P(None, "dp"), P(None, "dp", None))
        + (split,) * 7
        + (P("section", "dp"),) * 2,
        out_specs=(P("section", None, "dp", None),) * 2
        + (split,) * 7
        + (P("section", "dp"),) * 2,
        check_vma=False,
    )
```

```python
from functools import partial

import jax
import jax.numpy as jnp
from jax import lax
from jax.experimental import pallas as pl
from jax.experimental.pallas import tpu as pltpu
from jax.sharding import PartitionSpec as P

D = 960
HEADS = 15
KV_HEADS = 5
GROUP = HEADS // KV_HEADS
HEAD_DIM = 64
FF = 2560
QD = 960
KVD = 320
OWNERS = 64
SLOT = 15
PADDED = 16
DOWN_ROWS = 40

norm_eps = 1e-05
masked_score = -1e30
rope_base = 10000.0

f32 = jnp.float32
bf16 = jnp.bfloat16


def gray(value):
    return value ^ (value >> 1)


AXIS_SHIFT = {"y": 4, "z": 2, "x": 0}
BITS = (("y", 1), ("y", 0), ("z", 1), ("z", 0), ("x", 1), ("x", 0))


def partner_pairs(bit):
    axis, place = bit
    shift = AXIS_SHIFT[axis]
    pairs = []
    for source in range(OWNERS):
        coordinate = (source >> shift) & 3
        other = gray(gray(coordinate) ^ (1 << place))
        pairs.append((source, source + ((other - coordinate) << shift)))
    return pairs


def owner_of(position):
    me = lax.axis_index("dp")
    owner = 0
    for shift in (4, 2, 0):
        owner = owner + (gray(gray((me >> shift) & 3) ^ ((position >> shift) & 3)) << shift)
    return owner


def dot(left, right):
    return jnp.dot(left, right, preferred_element_type=f32)


def dot_t(left, right):
    return lax.dot_general(left, right, (((1,), (1,)), ((), ())), preferred_element_type=f32)


def spread_matrix():
    row = lax.broadcasted_iota(jnp.int32, (D, OWNERS * PADDED), 0)
    col = lax.broadcasted_iota(jnp.int32, (D, OWNERS * PADDED), 1)
    return ((row == SLOT * (col // PADDED) + col % PADDED) & (col % PADDED < SLOT)).astype(bf16)


def own_spread():
    row = lax.broadcasted_iota(jnp.int32, (OWNERS * PADDED, D), 0)
    col = lax.broadcasted_iota(jnp.int32, (OWNERS * PADDED, D), 1)
    owner = owner_of(row // PADDED)
    return ((col == SLOT * owner + row % PADDED) & (row % PADDED < SLOT)).astype(bf16)


CHUNK = 128
CHUNKS = 8
KV_CHUNKS = 3
PIECES = ((0, 960), (960, 1920), (1920, 2560))
SLABS = 8
VMEM_BYTES = 20 * 2**20
FORWARD_BYTES = 34 * 2**20
FEED_BYTES = 36 * 2**20
ATTENTION_BYTES = 20 * 2**20


def mm(left, right):
    return lax.dot_general(left, right, (((1,), (0,)), ((), ())), preferred_element_type=f32)


def mm_t(left, right):
    return lax.dot_general(left, right, (((1,), (1,)), ((), ())), preferred_element_type=f32)


def mm_tl(left, right):
    return lax.dot_general(left, right, (((0,), (0,)), ((), ())), preferred_element_type=f32)


def lanes(shape):
    return lax.broadcasted_iota(jnp.int32, shape, len(shape) - 1)


def cut_chunk(value, index):
    width = value.shape[1]
    low = index * CHUNK
    high = min(low + CHUNK, width)
    part = value[:, low:high]
    if high - low < CHUNK:
        part = jnp.concatenate(
            [part, jnp.zeros((value.shape[0], CHUNK - (high - low)), value.dtype)], axis=1
        )
    return part


def turn(value, cosine, sine):
    first = lanes(value.shape) % HEAD_DIM < HEAD_DIM // 2
    swapped = jnp.where(
        first, pltpu.roll(value, CHUNK - HEAD_DIM // 2, 1), pltpu.roll(value, HEAD_DIM // 2, 1)
    )
    return value * cosine + swapped * sine


def doubled(chunk, half):
    other = pltpu.roll(chunk, HEAD_DIM, 1)
    low = lanes(chunk.shape) < HEAD_DIM
    return jnp.where(low, chunk, other) if half == 0 else jnp.where(low, other, chunk)


def only(chunk, half):
    keep = (lanes(chunk.shape) < HEAD_DIM) == (half == 0)
    return jnp.where(keep, chunk, jnp.zeros_like(chunk))


class Loader:
    def __init__(self, big_ref, slabs, down, sems, order):
        self.slabs, self.down, self.copies = slabs, down, {}
        self.places = {index: place for place, index in enumerate(i for i in order if i < SLABS)}
        for index in order:
            if index < SLABS:
                source = big_ref.at[:, pl.ds(PADDED * index, PADDED), :]
                target = slabs.at[self.places[index]]
            else:
                low, high = (bound // DOWN_ROWS for bound in PIECES[index - SLABS])
                source = big_ref.at[low:high, PADDED * SLABS :, :]
                target = down.at[low:high]
            self.copies[index] = pltpu.make_async_copy(source, target, sems.at[index])
            self.copies[index].start()

    def need(self, index):
        self.copies[index].wait()

    def __getitem__(self, index):
        return self.slabs[self.places[index]]

    def down_rows(self, piece):
        low, high = PIECES[piece]
        return self.down[low // DOWN_ROWS : high // DOWN_ROWS].reshape(high - low, D)


def slab(slabs, index, low=0, high=D):
    return slabs[index].reshape(OWNERS * PADDED, D)[:, low:high]


def gate_slab(slabs, piece):
    return slab(slabs, 2 + piece) if piece < 2 else slab(slabs, 6, 0, 640)


def up_slab(slabs, piece):
    return slab(slabs, 4 + piece) if piece < 2 else slab(slabs, 7, 0, 640)


def unit_rows(value):
    inverse = lax.rsqrt(jnp.mean(value * value, axis=-1, keepdims=True) + norm_eps)
    return value * inverse, inverse


def forward_kernel(
    x_ref, cos_ref, sin_ref, allow_ref, live_ref, gains_ref, spread_ref, big_ref,
    y_ref, q_ref, k_ref, v_ref, p_ref, o_ref, m_ref, g0_ref, g1_ref, g2_ref, u0_ref, u1_ref, u2_ref,
    slabs, down, sems,
):
    weights = Loader(big_ref, slabs, down, sems, (0, 6, 7, 1, 2, 4, 3, 5, 8, 9, 10))
    cosine, sine = cos_ref[...], sin_ref[...]
    allowed = allow_ref[...] > 0
    spread = spread_ref[...]
    h = x_ref[...].astype(f32)
    n1, _ = unit_rows(h)
    a = (n1 * gains_ref[0:1, :]).astype(bf16)
    a_wide = mm(a, spread).astype(bf16)
    weights.need(0)
    q_all = mm(a_wide, slab(weights, 0))
    weights.need(6)
    k_all = mm(a_wide, slab(weights, 6, 640, 960))
    weights.need(7)
    v_all = mm(a_wide, slab(weights, 7, 640, 960))
    keys, values = [], []
    for index in range(KV_CHUNKS):
        k_chunk = turn(cut_chunk(k_all, index), cosine, sine)
        v_chunk = cut_chunk(v_all, index)
        k_ref[index] = k_chunk.astype(bf16)
        v_ref[index] = v_chunk.astype(bf16)
        for half in range(2):
            keys.append(doubled(k_chunk, half).astype(bf16))
            values.append(doubled(v_chunk, half).astype(bf16))
    mixed = []
    for index in range(CHUNKS):
        q_chunk = turn(cut_chunk(q_all, index), cosine, sine).astype(bf16)
        q_ref[index] = q_chunk
        total = None
        for half in range(2):
            head = 2 * index + half
            if head >= HEADS:
                continue
            s = mm_t(only(q_chunk, half), keys[head // GROUP]) * HEAD_DIM**-0.5
            s = jnp.where(allowed, s, masked_score)
            e = jnp.exp(s - jnp.max(s, axis=-1, keepdims=True))
            p = e / jnp.sum(e, axis=-1, keepdims=True)
            p_ref[head] = p
            part = mm(p.astype(bf16), only(values[head // GROUP], half))
            total = part if total is None else total + part
        mixed.append(total)
    o = jnp.concatenate(mixed, axis=1)[:, :QD].astype(bf16)
    o_ref[...] = o
    o_wide = mm(o, spread).astype(bf16)
    weights.need(1)
    m = h + mm(o_wide, slab(weights, 1))
    m_ref[...] = m
    n2, _ = unit_rows(m)
    b = (n2 * gains_ref[1:2, :]).astype(bf16)
    b_wide = mm(b, spread).astype(bf16)
    hiddens = []
    for piece, (g_ref, u_ref) in enumerate(((g0_ref, u0_ref), (g1_ref, u1_ref), (g2_ref, u2_ref))):
        if piece < 2:
            weights.need(2 + piece)
            weights.need(4 + piece)
        gate = mm(b_wide, gate_slab(weights, piece))
        up = mm(b_wide, up_slab(weights, piece))
        g_ref[...] = gate
        u_ref[...] = up
        hiddens.append((gate * lax.logistic(gate) * up).astype(bf16))
    total = m
    for piece, hidden in enumerate(hiddens):
        weights.need(SLABS + piece)
        total = total + mm(hidden, weights.down_rows(piece))
    y_ref[...] = (total * live_ref[...]).astype(bf16)


def narrow(value, spread):
    high = value.astype(bf16)
    low = (value - high.astype(f32)).astype(bf16)
    both = mm_t(jnp.concatenate([high, low], axis=0), spread)
    return both[: value.shape[0]] + both[value.shape[0] :]


def norm_grad(grad, normal, inverse, gain):
    scaled = grad * gain
    inner = jnp.mean(scaled * normal, axis=-1, keepdims=True)
    return inverse * (scaled - normal * inner)


def feed_forward_back_kernel(
    top_ref, m_ref, live_ref, gains_ref,
    g0_far, g1_far, g2_far, u0_far, u1_far, u2_far, spread_far, big_ref,
    dm_ref, low_ref, d3_ref, dg0_ref, dg1_ref, dg2_ref, du0_ref, du1_ref, du2_ref,
    dgain_ref, b_ref, h0_ref, h1_ref, h2_ref,
    slabs, down, sems,
    g0_ref, g1_ref, g2_ref, u0_ref, u1_ref, u2_ref, spread_ref, near_sems,
):
    far = (g0_far, u0_far, g1_far, u1_far, g2_far, u2_far, spread_far)
    near = (g0_ref, u0_ref, g1_ref, u1_ref, g2_ref, u2_ref, spread_ref)
    brought = [
        pltpu.make_async_copy(source, target, near_sems.at[index])
        for index, (source, target) in enumerate(zip(far, near))
    ]
    for copy in brought[:2]:
        copy.start()
    weights = Loader(big_ref, slabs, down, sems, (8, 2, 4, 9, 3, 5, 10, 6, 7))
    for copy in brought[2:]:
        copy.start()
    gain_f = gains_ref[1:2, :]
    d3 = top_ref[...].astype(f32) * live_ref[...]
    d3_low = d3.astype(bf16)
    d3_ref[...] = d3_low
    n2, r2 = unit_rows(m_ref[...])
    b_ref[...] = (n2 * gain_f).astype(bf16)
    wide = jnp.zeros((d3.shape[0], OWNERS * PADDED), f32)
    refs = (
        (g0_ref, u0_ref, dg0_ref, du0_ref, h0_ref),
        (g1_ref, u1_ref, dg1_ref, du1_ref, h1_ref),
        (g2_ref, u2_ref, dg2_ref, du2_ref, h2_ref),
    )
    for piece, (g_ref, u_ref, dg_ref, du_ref, hid_ref) in enumerate(refs):
        weights.need(SLABS + piece)
        dhidden = mm_t(d3_low, weights.down_rows(piece))
        brought[2 * piece].wait()
        brought[2 * piece + 1].wait()
        gate, up = g_ref[...], u_ref[...]
        sig = lax.logistic(gate)
        act = gate * sig
        hid_ref[...] = (act * up).astype(bf16)
        dg = (dhidden * up * sig * (1.0 + gate * (1.0 - sig))).astype(bf16)
        du = (dhidden * act).astype(bf16)
        dg_ref[...] = dg
        du_ref[...] = du
        if piece < 2:
            weights.need(2 + piece)
            weights.need(4 + piece)
        else:
            weights.need(6)
            weights.need(7)
        wide = wide + mm_t(dg, gate_slab(weights, piece)) + mm_t(du, up_slab(weights, piece))
    brought[6].wait()
    db = narrow(wide, spread_ref[...])
    dgain_ref[...] = jnp.sum(db * n2, axis=0, keepdims=True)
    dm = d3 + norm_grad(db, n2, r2, gain_f)
    dm_ref[...] = dm
    low_ref[...] = dm.astype(bf16)


def attention_back_kernel(
    x_ref, dm_ref, low_ref, q_ref, k_ref, v_ref, p_ref,
    cos_ref, sin_ref, gains_ref, spread_ref, big_ref,
    dh_ref, dq_ref, dk_ref, dv_ref, dgain_ref, a_ref,
    slabs, sems,
):
    weights = Loader(big_ref, slabs, None, sems, (1, 0, 6, 7))
    cosine, sine = cos_ref[...], sin_ref[...]
    spread = spread_ref[...]
    gain_a = gains_ref[0:1, :]
    weights.need(1)
    do = mm_t(mm_t(low_ref[...], slab(weights, 1)).astype(bf16), spread).astype(bf16)
    keys, values = [], []
    for index in range(KV_CHUNKS):
        k_chunk, v_chunk = k_ref[index].astype(f32), v_ref[index].astype(f32)
        for half in range(2):
            keys.append(doubled(k_chunk, half).astype(bf16))
            values.append(doubled(v_chunk, half).astype(bf16))
    dk_sums, dv_sums = [None] * KV_HEADS, [None] * KV_HEADS
    dq_parts = []
    for index in range(CHUNKS):
        do_chunk = cut_chunk(do, index)
        q_chunk = q_ref[index]
        total = None
        for half in range(2):
            head = 2 * index + half
            if head >= HEADS:
                continue
            group = head // GROUP
            do_head, q_head = only(do_chunk, half), only(q_chunk, half)
            p = p_ref[head]
            dp = mm_t(do_head, values[group])
            dv = mm_tl(p.astype(bf16), do_head)
            ds = (p * (dp - jnp.sum(p * dp, axis=-1, keepdims=True))).astype(bf16)
            dk = mm_tl(ds, q_head)
            part = mm(ds, only(keys[group], half))
            total = part if total is None else total + part
            dk_sums[group] = dk if dk_sums[group] is None else dk_sums[group] + dk
            dv_sums[group] = dv if dv_sums[group] is None else dv_sums[group] + dv
        dq_parts.append(turn(total * HEAD_DIM**-0.5, cosine, -sine))
    dq = jnp.concatenate(dq_parts, axis=1)[:, :QD].astype(bf16)
    low_lanes = lanes((do.shape[0], CHUNK)) < HEAD_DIM
    dk_parts, dv_parts = [], []
    for index in range(KV_CHUNKS):
        both = []
        for sums in (dk_sums, dv_sums):
            halves = []
            for half in range(2):
                group = 2 * index + half
                if group < KV_HEADS:
                    halves.append(sums[group] + pltpu.roll(sums[group], HEAD_DIM, 1))
                else:
                    halves.append(jnp.zeros_like(sums[0]))
            both.append(jnp.where(low_lanes, halves[0], halves[1]))
        dk_parts.append(turn(both[0] * HEAD_DIM**-0.5, cosine, -sine))
        dv_parts.append(both[1])
    dk = jnp.concatenate(dk_parts, axis=1)[:, :KVD].astype(bf16)
    dv = jnp.concatenate(dv_parts, axis=1)[:, :KVD].astype(bf16)
    dq_ref[...] = dq
    dk_ref[...] = dk
    dv_ref[...] = dv
    h = x_ref[...].astype(f32)
    n1, r1 = unit_rows(h)
    a_ref[...] = (n1 * gain_a).astype(bf16)
    weights.need(0)
    weights.need(6)
    weights.need(7)
    wide = (
        mm_t(dq, slab(weights, 0))
        + mm_t(dk, slab(weights, 6, 640, 960))
        + mm_t(dv, slab(weights, 7, 640, 960))
    )
    da = narrow(wide, spread)
    dgain_ref[...] = jnp.sum(da * n1, axis=0, keepdims=True)
    dh = dm_ref[...] + norm_grad(da, n1, r1, gain_a)
    dh_ref[...] = dh.astype(bf16)


def takes(microseconds):
    return pl.CostEstimate(
        flops=int(microseconds * 1.1e9), bytes_accessed=int(microseconds * 1e6), transcendentals=0
    )


def specs(count, anywhere=0):
    return [pl.BlockSpec(memory_space=pltpu.VMEM)] * count + [
        pl.BlockSpec(memory_space=pltpu.HBM)
    ] * anywhere


def weight_scratch(slabs):
    return [
        pltpu.VMEM((slabs, OWNERS, PADDED, D), bf16),
        pltpu.VMEM((OWNERS, DOWN_ROWS, D), bf16),
        pltpu.SemaphoreType.DMA((SLABS + len(PIECES),)),
    ]


def shapes(entries):
    return [jax.ShapeDtypeStruct(shape, kind) for shape, kind in entries]


def forward(x, tables, gains, spread, big):
    cosine, sine, allowed, live = tables
    rows = x.shape[0]
    widths = [high - low for low, high in PIECES]
    out = shapes(
        [
            ((rows, D), bf16),
            ((CHUNKS, rows, CHUNK), bf16),
            ((KV_CHUNKS, rows, CHUNK), bf16),
            ((KV_CHUNKS, rows, CHUNK), bf16),
            ((HEADS, rows, rows), f32),
            ((rows, QD), bf16),
            ((rows, D), f32),
        ]
    ) + [pltpu.HBM((rows, width), f32) for width in widths * 2]
    return pl.pallas_call(
        forward_kernel,
        out_shape=out,
        in_specs=specs(7, 1),
        out_specs=specs(len(out)),
        scratch_shapes=weight_scratch(8),
        compiler_params=pltpu.CompilerParams(vmem_limit_bytes=FORWARD_BYTES),
        name="layer_forward",
        cost_estimate=takes(13),
    )(x, cosine, sine, allowed, live, gains, spread, big)


def feed_forward_back(top, saved, tables, gains, spread, big):
    live = tables[3]
    rows = top.shape[0]
    widths = [high - low for low, high in PIECES]
    out = shapes(
        [((rows, D), f32), ((rows, D), bf16), ((rows, D), bf16)]
        + [((rows, width), bf16) for width in widths * 2]
        + [((1, D), f32), ((rows, D), bf16)]
        + [((rows, width), bf16) for width in widths]
    )
    far = [pltpu.with_memory_space_constraint(v, pltpu.HBM) for v in (*saved[6:], spread)]
    return pl.pallas_call(
        feed_forward_back_kernel,
        out_shape=out,
        in_specs=specs(4, 8),
        out_specs=specs(len(out)),
        scratch_shapes=weight_scratch(6)
        + [pltpu.VMEM((rows, width), f32) for width in widths * 2]
        + [pltpu.VMEM(spread.shape, bf16), pltpu.SemaphoreType.DMA((7,))],
        compiler_params=pltpu.CompilerParams(vmem_limit_bytes=FEED_BYTES),
        name="feed_forward_back",
        cost_estimate=takes(14),
    )(top, saved[5], live, gains, *far, big)


def attention_back(x, dm, dm_low, saved, tables, gains, spread, big):
    cosine, sine, _, _ = tables
    rows = x.shape[0]
    out = shapes(
        [((rows, D), bf16), ((rows, QD), bf16), ((rows, KVD), bf16), ((rows, KVD), bf16)]
        + [((1, D), f32), ((rows, D), bf16)]
    )
    scratch = weight_scratch(4)
    return pl.pallas_call(
        attention_back_kernel,
        out_shape=out,
        in_specs=specs(11, 1),
        out_specs=specs(len(out)),
        scratch_shapes=[scratch[0], scratch[2]],
        compiler_params=pltpu.CompilerParams(vmem_limit_bytes=ATTENTION_BYTES),
        name="attention_back",
        cost_estimate=takes(11.5),
    )(x, dm, dm_low, *saved[:4], cosine, sine, gains, spread, big)


def tables_of(starts):
    micro, rows = starts.shape
    local = jnp.arange(rows, dtype=jnp.int32)
    live = (starts <= local).reshape(-1)
    position = jnp.where(starts <= local, local - starts, 0).astype(f32).reshape(-1, 1)
    lane = jnp.arange(CHUNK, dtype=jnp.int32)
    turn_index = (lane % (HEAD_DIM // 2)).astype(f32)
    angles = position * rope_base ** (-2.0 * turn_index / HEAD_DIM)
    sign = jnp.where(lane % HEAD_DIM < HEAD_DIM // 2, -1.0, 1.0).astype(f32)
    row = jnp.arange(micro * rows, dtype=jnp.int32)
    begin = starts.reshape(-1, 1)
    column = row[None, :]
    same = (row[:, None] // rows) == (column // rows)
    inside = (column % rows >= begin) & (column <= row[:, None])
    allowed = (same & inside) | (row[:, None] == column)
    return jnp.cos(angles), jnp.sin(angles) * sign, allowed.astype(f32), live.astype(f32)[:, None]


STREAM_KINDS = (("a", "gain"), ("b",), ("b",), ("h0", "h1"), ("o", "h2"))
STREAM_RIGHTS = (14, 20, 20, 8, 16)
STREAM_CHUNKS = (14, 20, 20, 16, 12)
LEFT_ROWS = OWNERS // 2 * PADDED


def rotations(place, then):
    axes = "yzx"
    result = []
    for turned in (axes[start:] + axes[:start] for start in range(3)):
        result.append(
            tuple((axis, place) for axis in turned) + tuple((axis, then) for axis in turned)
        )
    return result


HIGH_FIRST, LOW_FIRST = rotations(1, 0), rotations(0, 1)
ORDERS = (HIGH_FIRST[0], LOW_FIRST[0], LOW_FIRST[1], HIGH_FIRST[1], HIGH_FIRST[2])
GROUPS = ((0, 3, 4), (1, 2))


def split_bit(value, dim, bits):
    shape = value.shape[1:]
    view = value.reshape((2**dim, 2, 2 ** (bits - 1 - dim)) + shape)
    return [view[:, index].reshape((2 ** (bits - 1),) + shape) for index in (0, 1)]


def chunks_of(value):
    count = (value.shape[1] + CHUNK - 1) // CHUNK
    return [cut_chunk(value, index) for index in range(count)]


def write_stream(stream, lefts, rights, keep_ref, pack_ref):
    rows = rights[0].shape[0]
    dim = BITS.index(ORDERS[stream][0])
    base = 0
    for index, left in enumerate(lefts):
        kept, sent = split_bit(left, dim, 6)
        keep_ref[index] = kept
        pack_ref[base : base + LEFT_ROWS, :] = sent.reshape(LEFT_ROWS, rows)
        base += LEFT_ROWS
    for chunk in rights:
        pack_ref[base : base + rows, :] = chunk
        base += rows


def in_order(mine, value):
    return mm_t(mine, value).astype(bf16).reshape(OWNERS, PADDED, value.shape[0])


def late_operand_kernel(
    mine_ref, a_ref, attn_ref, ffn_ref, dq_ref, dk_ref, dv_ref, keep_ref, pack_ref
):
    mine = mine_ref[...]
    rows = a_ref.shape[0]
    gain = jnp.concatenate([attn_ref[...], ffn_ref[...], jnp.zeros((rows - 2, D), f32)], axis=0)
    lefts = in_order(mine, a_ref[...]), in_order(mine, gain.astype(bf16))
    dq, dk, dv = dq_ref[...], dk_ref[...], dv_ref[...]
    tail = jnp.concatenate([dq[:, 896:], dk[:, 256:]], axis=1)
    identity = lax.broadcasted_iota(jnp.int32, (rows, CHUNK), 0) == lanes((rows, CHUNK))
    rights = chunks_of(dq)[:7] + chunks_of(dk)[:2] + [tail] + chunks_of(dv)
    write_stream(0, lefts, rights + [identity.astype(f32).astype(bf16)], keep_ref, pack_ref)


def early_operand_kernel(
    owner_ref, mine_ref, b_ref, o_ref, h0_ref, h1_ref, h2_ref, dm_ref, d3_ref,
    dg0_ref, dg1_ref, dg2_ref, du0_ref, du1_ref, du2_ref,
    *rest,
):
    keeps, packs = rest[:4], rest[4:8]
    turned, lefts = rest[8:]
    mine = mine_ref[...]
    rows = b_ref.shape[0]

    hidden = jnp.concatenate([h0_ref[...], h1_ref[...], h2_ref[...]], axis=1).astype(f32)
    turned[...] = hidden.T.reshape(OWNERS, DOWN_ROWS, rows)

    @pl.loop(0, OWNERS)
    def _(place):
        block = turned[owner_ref[place]]
        lefts[0, place] = block[0:16].astype(bf16)
        lefts[1, place] = block[16:32].astype(bf16)
        lefts[2, place] = jnp.concatenate(
            [block[32:40], jnp.zeros((8, rows), f32)], axis=0
        ).astype(bf16)

    b = in_order(mine, b_ref[...])
    o = in_order(mine, o_ref[...])
    dg = jnp.concatenate([dg0_ref[...], dg1_ref[...], dg2_ref[...]], axis=1)
    du = jnp.concatenate([du0_ref[...], du1_ref[...], du2_ref[...]], axis=1)
    d3, dm = chunks_of(d3_ref[...]), chunks_of(dm_ref[...])
    write_stream(1, (b,), chunks_of(dg), keeps[0], packs[0])
    write_stream(2, (b,), chunks_of(du), keeps[1], packs[1])
    write_stream(3, (lefts[0], lefts[1]), d3, keeps[2], packs[2])
    write_stream(4, (o, lefts[2]), dm + d3, keeps[3], packs[3])


def operand_shapes(streams, rows):
    return shapes(
        [((len(STREAM_KINDS[s]), OWNERS // 2, PADDED, rows), bf16) for s in streams]
        + [
            ((len(STREAM_KINDS[s]) * LEFT_ROWS + STREAM_RIGHTS[s] * rows, CHUNK), bf16)
            for s in streams
        ]
    )


def early_operands(mine, b, o, hidden, dm_low, d3, dg, du):
    rows = b.shape[0]
    out = operand_shapes((1, 2, 3, 4), rows)
    owners = owner_of(jnp.arange(OWNERS, dtype=jnp.int32))
    result = pl.pallas_call(
        early_operand_kernel,
        out_shape=out,
        in_specs=[pl.BlockSpec(memory_space=pltpu.SMEM)] + specs(14),
        out_specs=specs(len(out)),
        scratch_shapes=[
            pltpu.VMEM((OWNERS, DOWN_ROWS, rows), f32),
            pltpu.VMEM((3, OWNERS, PADDED, rows), bf16),
        ],
        compiler_params=pltpu.CompilerParams(vmem_limit_bytes=VMEM_BYTES),
        name="early_operands",
        cost_estimate=takes(7),
    )(owners, mine, b, o, *hidden, dm_low, d3, *dg, *du)
    return result[:4], result[4:]


def late_operands(mine, a, dattn, dffn, dq, dk, dv):
    out = operand_shapes((0,), a.shape[0])
    return pl.pallas_call(
        late_operand_kernel,
        out_shape=out,
        in_specs=specs(7),
        out_specs=specs(2),
        compiler_params=pltpu.CompilerParams(vmem_limit_bytes=VMEM_BYTES),
        name="late_operands",
        cost_estimate=takes(4),
    )(mine, a, dattn, dffn, dq, dk, dv)


def product_kernel(streams, *refs):
    count = len(streams)
    keeps, packs, others = (
        dict(zip(streams, refs[count * part : count * (part + 1)])) for part in range(3)
    )
    outs = {s: refs[3 * count + 2 * i : 3 * count + 2 * i + 2] for i, s in enumerate(streams)}
    step = pl.program_id(0)

    def left_of(stream, kind):
        kept = keeps[stream][kind].reshape(LEFT_ROWS, CHUNK)
        window = pl.ds(kind * LEFT_ROWS, LEFT_ROWS)
        return jnp.concatenate([kept, others[stream][window, :]], axis=1)

    def right_of(stream, chunk):
        start = len(STREAM_KINDS[stream]) * LEFT_ROWS + chunk * CHUNK
        if not isinstance(start, int):
            start = pl.multiple_of(start, CHUNK)
        window = pl.ds(start, CHUNK)
        return jnp.concatenate([packs[stream][window, :], others[stream][window, :]], axis=0)

    def right_pair(stream, first, second):
        return jnp.concatenate([right_of(stream, first), right_of(stream, second)], axis=1)

    def blocks_of(value):
        return value.reshape(OWNERS // 2, PADDED, CHUNK)

    def store(stream, place, value):
        dim = [bit for bit in BITS if bit != ORDERS[stream][0]].index(ORDERS[stream][1])
        kept, sent = split_bit(value.astype(bf16), dim, 5)
        outs[stream][0][place] = kept
        outs[stream][1][place] = sent

    def usual(stream, kind, first):
        value = mm(left_of(stream, kind), right_pair(stream, first, first + 1))
        store(stream, 0, blocks_of(value[:, :CHUNK]))
        store(stream, 1, blocks_of(value[:, CHUNK:]))

    def short_rows(stream, kind, first):
        value = mm(left_of(stream, kind), right_pair(stream, first, first + 4))
        parts = [blocks_of(part)[:, :8] for part in (value[:, :CHUNK], value[:, CHUNK:])]
        return jnp.concatenate(parts, axis=1)

    def when(condition, action):
        pl.when(condition)(action)

    if 0 in streams:
        when(step < 6, lambda: usual(0, 0, 2 * step))

        @pl.when(step == 6)
        def _():
            store(0, 0, blocks_of(mm(left_of(0, 0), right_of(0, 12))))
            store(0, 1, blocks_of(mm(left_of(0, 1), right_of(0, 13))))

    if 1 in streams:
        usual(1, 0, 2 * step)
    if 2 in streams:
        usual(2, 0, 2 * step)
    if 3 in streams:
        when(step < 4, lambda: usual(3, 0, 2 * step))
        when(step >= 4, lambda: usual(3, 1, 2 * step - 8))
    if 4 in streams:
        when(step < 4, lambda: usual(4, 0, 2 * step))

        @pl.when((step >= 4) & (step < 6))
        def _():
            for place in range(2):
                store(4, place, short_rows(4, 1, 8 + 2 * (step - 4) + place))


def products(streams, keeps, packs, others):
    out, out_specs = [], []
    for stream in streams:
        last = STREAM_CHUNKS[stream] // 2 - 1
        for _ in range(2):
            out.append(((STREAM_CHUNKS[stream], OWNERS // 4, PADDED, CHUNK), bf16))
            out_specs.append(
                pl.BlockSpec(
                    (2, OWNERS // 4, PADDED, CHUNK),
                    lambda step, last=last: (jnp.minimum(step, last), 0, 0, 0),
                )
            )
    result = pl.pallas_call(
        partial(product_kernel, streams),
        grid=(max(STREAM_CHUNKS[stream] for stream in streams) // 2,),
        out_shape=shapes(out),
        in_specs=specs(3 * len(streams)),
        out_specs=out_specs,
        compiler_params=pltpu.CompilerParams(vmem_limit_bytes=VMEM_BYTES),
        name="grad_products",
        cost_estimate=takes(sum(STREAM_CHUNKS[stream] for stream in streams) * 0.2),
    )(*keeps, *packs, *others)
    return list(result[0::2]), list(result[1::2])


def together(values):
    return list(lax.optimization_barrier(tuple(values)))


def send(values, bits):
    return together([lax.ppermute(v, "dp", partner_pairs(b)) for v, b in zip(values, bits)])


def halved(kept, arrived, dim):
    size = kept.shape[1]
    view = (kept.shape[0], 2**dim, 2, size >> (dim + 1)) + kept.shape[2:]
    flat = (kept.shape[0], size // 2) + kept.shape[2:]
    first, second = kept.reshape(view), arrived.reshape(view)
    return tuple(
        (first[:, :, index].astype(f32) + second[:, :, index].astype(f32))
        .astype(bf16)
        .reshape(flat)
        for index in (0, 1)
    )


def exchanged(streams, packs):
    return send(packs, [ORDERS[stream][0] for stream in streams])


def three_steps(streams, keeps, packs, others):
    orders = [ORDERS[stream] for stream in streams]
    kept, sent = products(streams, keeps, packs, others)
    arrived = send(sent, [order[1] for order in orders])
    for index, order in enumerate(orders):
        left = [bit for bit in BITS if bit not in order[:2]]
        kept[index], sent[index] = halved(kept[index], arrived[index], left.index(order[2]))
    return kept, send(sent, [order[2] for order in orders])


def last_steps(parts):
    kept, sent, rest = [], [], []
    for members, (keeps, arrived) in zip(GROUPS, parts):
        order = ORDERS[members[0]]
        left = [bit for bit in BITS if bit not in order[:3]]
        halves = [halved(k, a, left.index(order[3])) for k, a in zip(keeps, arrived)]
        kept.append(jnp.concatenate([half[0] for half in halves], axis=0))
        sent.append(jnp.concatenate([half[1] for half in halves], axis=0))
        rest.append((left, order[3:]))
    for step in range(3):
        arrived = send(sent, [order[step] for _, order in rest])
        for group, (left, order) in enumerate(rest):
            left.remove(order[step])
            if step < 2:
                dim = left.index(order[step + 1])
                kept[group], sent[group] = halved(kept[group], arrived[group], dim)
    return kept, arrived


def result_kernel(
    kept0_ref, kept1_ref, came0_ref, came1_ref,
    query_ref, key_ref, value_ref, output_ref, gate_ref, up_ref, down_ref, attn_ref, ffn_ref,
):
    def block(group, index):
        kept, came = ((kept0_ref, came0_ref), (kept1_ref, came1_ref))[group]
        return kept[index, 0].astype(f32) + came[index, 0].astype(f32)

    def put(ref, low, high, value, column):
        width = min(CHUNK, ref.shape[-1] - column)
        value = value[: high - low, :width]
        if len(ref.shape) == 3:
            ref[low:high, 0, column : column + width] = value
        else:
            ref[low:high, column : column + width] = value

    half = HEAD_DIM
    for index in range(7):
        put(query_ref, 0, SLOT, block(0, index), CHUNK * index)
    for index in range(2):
        put(key_ref, 0, SLOT, block(0, 7 + index), CHUNK * index)
    tail = block(0, 9)
    put(query_ref, 0, SLOT, tail, 896)
    put(key_ref, 0, SLOT, tail[:, half:], 256)
    for index in range(3):
        put(value_ref, 0, SLOT, block(0, 10 + index), CHUNK * index)
    gains = block(0, 13)
    eye = (lax.broadcasted_iota(jnp.int32, (8, CHUNK), 0) == lanes((8, CHUNK))).astype(f32)
    turned = lax.dot_general(
        eye, gains, (((1,), (1,)), ((), ())),
        preferred_element_type=f32, precision=lax.Precision.HIGHEST,
    )
    attn_ref[...] = turned[0:1, :SLOT]
    ffn_ref[...] = turned[1:2, :SLOT]
    for index in range(8):
        put(down_ref, 0, 16, block(0, 14 + index), CHUNK * index)
        put(down_ref, 16, 32, block(0, 22 + index), CHUNK * index)
        put(output_ref, 0, SLOT, block(0, 30 + index), CHUNK * index)
    for index in range(4):
        both = block(0, 38 + index)
        put(down_ref, 32, 40, both[:8], CHUNK * index)
        put(down_ref, 32, 40, both[8:], CHUNK * (index + 4))
    for index in range(20):
        put(gate_ref, 0, SLOT, block(1, index), CHUNK * index)
        put(up_ref, 0, SLOT, block(1, 20 + index), CHUNK * index)


def weight_results(kept, came):
    wide = [(SLOT, 1, width) for width in (QD, KVD, KVD, D, FF, FF)]
    out = shapes([(shape, f32) for shape in wide + [(DOWN_ROWS, D), (1, SLOT), (1, SLOT)]])
    result = pl.pallas_call(
        result_kernel,
        out_shape=out,
        in_specs=specs(4),
        out_specs=specs(len(out)),
        name="weight_results",
        cost_estimate=takes(3),
    )(*kept, *came)
    slots = tuple(value.transpose(1, 0, 2) for value in result[:6])
    return slots + (result[6][None],) + tuple(result[7:])


def pack_kernel(q_ref, k_ref, v_ref, o_ref, g_ref, u_ref, d_ref, gain_ref, out_ref):
    blank = jnp.zeros((PADDED - SLOT, D), bf16)
    g, u = g_ref[0], u_ref[0]
    plain = (
        q_ref[0],
        o_ref[0],
        g[:, :960],
        g[:, 960:1920],
        u[:, :960],
        u[:, 960:1920],
        jnp.concatenate([g[:, 1920:], k_ref[0]], axis=1),
        jnp.concatenate([u[:, 1920:], v_ref[0]], axis=1),
    )
    for index, value in enumerate(plain):
        last = gain_ref[...] if index == 0 else blank
        full = jnp.concatenate([value.astype(f32), last.astype(f32)], axis=0)
        out_ref[0, PADDED * index : PADDED * (index + 1), :] = full.astype(bf16)
    out_ref[0, PADDED * SLABS :, :] = d_ref[0]


def packed_weights(w_query, w_key, w_value, w_output, w_gate, w_up, w_down, attn_gain, ffn_gain):
    gains = jnp.concatenate([attn_gain, ffn_gain], axis=1)
    gain_row = jnp.pad(gains, ((0, 0), (0, D - gains.shape[1])))
    return pl.pallas_call(
        pack_kernel,
        out_shape=jax.ShapeDtypeStruct((1, PADDED * SLABS + DOWN_ROWS, D), bf16),
        in_specs=specs(8),
        out_specs=pl.BlockSpec(memory_space=pltpu.VMEM),
        name="pack_weights",
        cost_estimate=takes(2),
    )(w_query, w_key, w_value, w_output, w_gate, w_up, w_down, gain_row)


def body(inputs, starts, cotangent, *weights):
    section = lax.axis_index("section")
    micro, rows = starts.shape
    everything = lax.all_gather(packed_weights(*weights), "dp", axis=0, tiled=True)
    everything, spread, mine, *tables = together(
        [everything, spread_matrix(), own_spread(), *tables_of(starts)]
    )
    all_gains = everything[:, SLOT, : 2 * SLOT].astype(f32)
    all_gains = jnp.stack([all_gains[:, :SLOT].reshape(D), all_gains[:, SLOT:].reshape(D)])
    first_in = inputs.reshape(micro * rows, D)
    top = cotangent.reshape(micro * rows, D)
    everything = pltpu.with_memory_space_constraint(everything, pltpu.HBM)
    shared = (tables, all_gains, spread, everything)

    made = forward(first_in, *shared)[0]
    arrived = lax.ppermute(made, "section", [(0, 1)])
    source = jnp.where(section == 0, first_in, arrived)
    result, *saved = forward(source, *shared)

    dm, dm_low = feed_forward_back(top, saved, *shared)[:2]
    back = attention_back(source, dm, dm_low, saved, *shared)[0]
    returned = lax.ppermute(back, "section", [(1, 0)])
    upstream = jnp.where(section == 1, top, returned)

    ffn = feed_forward_back(upstream, saved, *shared)
    dm, dm_low, d3, dffn, b, hidden = ffn[0], ffn[1], ffn[2], ffn[9], ffn[10], ffn[11:14]
    keeps, packs = early_operands(mine, b, saved[4], hidden, dm_low, d3, ffn[3:6], ffn[6:9])
    dm, dm_low, *packs = together([dm, dm_low, *packs])
    others = exchanged((1, 2, 3, 4), packs)
    grad_rows, dq, dk, dv, dattn, a = attention_back(source, dm, dm_low, saved, *shared)
    a, *others = together([a, *others])
    late_keep, late_pack = late_operands(mine, a, dattn, dffn, dq, dk, dv)
    last = exchanged((0,), [late_pack])

    gate_up = three_steps((1, 2), keeps[:2], packs[:2], others[:2])
    down_out = three_steps((3, 4), keeps[2:], packs[2:], others[2:])
    query = three_steps((0,), [late_keep], [late_pack], last)
    first_group = (query[0] + down_out[0], query[1] + down_out[1])
    sums = weight_results(*last_steps((first_group, gate_up)))
    rows_out = (result.reshape(1, micro, rows, D), grad_rows.reshape(1, micro, rows, D))
    return rows_out + sums


def solution(mesh):
    split = P("section", "dp", None)
    return jax.shard_map(
        body,
        mesh=mesh,
        in_specs=(P(None, "dp", None), P(None, "dp"), P(None, "dp", None))
        + (split,) * 7
        + (P("section", "dp"),) * 2,
        out_specs=(P("section", None, "dp", None),) * 2
        + (split,) * 7
        + (P("section", "dp"),) * 2,
        check_vma=False,
    )
```

```python
from functools import partial

import jax
import jax.numpy as jnp
from jax import lax
from jax.experimental import pallas as pl
from jax.experimental.pallas import tpu as pltpu
from jax.sharding import PartitionSpec as P

D = 960
HEADS = 15
KV_HEADS = 5
GROUP = HEADS // KV_HEADS
HEAD_DIM = 64
FF = 2560
QD = 960
KVD = 320
OWNERS = 64
SLOT = 15
PADDED = 16
DOWN_ROWS = 40

norm_eps = 1e-05
masked_score = -1e30
rope_base = 10000.0

f32 = jnp.float32
bf16 = jnp.bfloat16


def gray(value):
    return value ^ (value >> 1)


AXIS_SHIFT = {"y": 4, "z": 2, "x": 0}
BITS = (("y", 1), ("y", 0), ("z", 1), ("z", 0), ("x", 1), ("x", 0))


def partner_pairs(bit):
    axis, place = bit
    shift = AXIS_SHIFT[axis]
    pairs = []
    for source in range(OWNERS):
        coordinate = (source >> shift) & 3
        other = gray(gray(coordinate) ^ (1 << place))
        pairs.append((source, source + ((other - coordinate) << shift)))
    return pairs


def owner_of(position):
    me = lax.axis_index("dp")
    owner = 0
    for shift in (4, 2, 0):
        owner = owner + (gray(gray((me >> shift) & 3) ^ ((position >> shift) & 3)) << shift)
    return owner


def dot(left, right):
    return jnp.dot(left, right, preferred_element_type=f32)


def dot_t(left, right):
    return lax.dot_general(left, right, (((1,), (1,)), ((), ())), preferred_element_type=f32)


def spread_matrix():
    row = lax.broadcasted_iota(jnp.int32, (D, OWNERS * PADDED), 0)
    col = lax.broadcasted_iota(jnp.int32, (D, OWNERS * PADDED), 1)
    return ((row == SLOT * (col // PADDED) + col % PADDED) & (col % PADDED < SLOT)).astype(bf16)


def own_spread():
    row = lax.broadcasted_iota(jnp.int32, (OWNERS * PADDED, D), 0)
    col = lax.broadcasted_iota(jnp.int32, (OWNERS * PADDED, D), 1)
    owner = owner_of(row // PADDED)
    return ((col == SLOT * owner + row % PADDED) & (row % PADDED < SLOT)).astype(bf16)


CHUNK = 128
CHUNKS = 8
KV_CHUNKS = 3
PIECES = ((0, 960), (960, 1920), (1920, 2560))
SLABS = 8
VMEM_BYTES = 20 * 2**20
FORWARD_BYTES = 34 * 2**20
FEED_BYTES = 36 * 2**20
ATTENTION_BYTES = 20 * 2**20


def mm(left, right):
    return lax.dot_general(left, right, (((1,), (0,)), ((), ())), preferred_element_type=f32)


def mm_t(left, right):
    return lax.dot_general(left, right, (((1,), (1,)), ((), ())), preferred_element_type=f32)


def mm_tl(left, right):
    return lax.dot_general(left, right, (((0,), (0,)), ((), ())), preferred_element_type=f32)


def lanes(shape):
    return lax.broadcasted_iota(jnp.int32, shape, len(shape) - 1)


def cut_chunk(value, index):
    width = value.shape[1]
    low = index * CHUNK
    high = min(low + CHUNK, width)
    part = value[:, low:high]
    if high - low < CHUNK:
        part = jnp.concatenate(
            [part, jnp.zeros((value.shape[0], CHUNK - (high - low)), value.dtype)], axis=1
        )
    return part


def turn(value, cosine, sine):
    first = lanes(value.shape) % HEAD_DIM < HEAD_DIM // 2
    swapped = jnp.where(
        first, pltpu.roll(value, CHUNK - HEAD_DIM // 2, 1), pltpu.roll(value, HEAD_DIM // 2, 1)
    )
    return value * cosine + swapped * sine


def doubled(chunk, half):
    other = pltpu.roll(chunk, HEAD_DIM, 1)
    low = lanes(chunk.shape) < HEAD_DIM
    return jnp.where(low, chunk, other) if half == 0 else jnp.where(low, other, chunk)


def only(chunk, half):
    keep = (lanes(chunk.shape) < HEAD_DIM) == (half == 0)
    return jnp.where(keep, chunk, jnp.zeros_like(chunk))


class Loader:
    def __init__(self, big_ref, slabs, down, sems, order):
        self.slabs, self.down, self.copies = slabs, down, {}
        self.places = {index: place for place, index in enumerate(i for i in order if i < SLABS)}
        for index in order:
            if index < SLABS:
                source = big_ref.at[:, pl.ds(PADDED * index, PADDED), :]
                target = slabs.at[self.places[index]]
            else:
                low, high = (bound // DOWN_ROWS for bound in PIECES[index - SLABS])
                source = big_ref.at[low:high, PADDED * SLABS :, :]
                target = down.at[low:high]
            self.copies[index] = pltpu.make_async_copy(source, target, sems.at[index])
            self.copies[index].start()

    def need(self, index):
        self.copies[index].wait()

    def __getitem__(self, index):
        return self.slabs[self.places[index]]

    def down_rows(self, piece):
        low, high = PIECES[piece]
        return self.down[low // DOWN_ROWS : high // DOWN_ROWS].reshape(high - low, D)


def slab(slabs, index, low=0, high=D):
    return slabs[index].reshape(OWNERS * PADDED, D)[:, low:high]


def gate_slab(slabs, piece):
    return slab(slabs, 2 + piece) if piece < 2 else slab(slabs, 6, 0, 640)


def up_slab(slabs, piece):
    return slab(slabs, 4 + piece) if piece < 2 else slab(slabs, 7, 0, 640)


def unit_rows(value):
    inverse = lax.rsqrt(jnp.mean(value * value, axis=-1, keepdims=True) + norm_eps)
    return value * inverse, inverse


def forward_kernel(
    x_ref, cos_ref, sin_ref, allow_ref, live_ref, gains_ref, spread_ref, big_ref,
    y_ref, q_ref, k_ref, v_ref, p_ref, o_ref, m_ref, g0_ref, g1_ref, g2_ref, u0_ref, u1_ref, u2_ref,
    slabs, down, sems,
):
    weights = Loader(big_ref, slabs, down, sems, (0, 6, 7, 1, 2, 4, 3, 5, 8, 9, 10))
    cosine, sine = cos_ref[...], sin_ref[...]
    allowed = allow_ref[...] > 0
    spread = spread_ref[...]
    h = x_ref[...].astype(f32)
    n1, _ = unit_rows(h)
    a = (n1 * gains_ref[0:1, :]).astype(bf16)
    a_wide = mm(a, spread).astype(bf16)
    weights.need(0)
    q_all = mm(a_wide, slab(weights, 0))
    weights.need(6)
    k_all = mm(a_wide, slab(weights, 6, 640, 960))
    weights.need(7)
    v_all = mm(a_wide, slab(weights, 7, 640, 960))
    keys, values = [], []
    for index in range(KV_CHUNKS):
        k_chunk = turn(cut_chunk(k_all, index), cosine, sine)
        v_chunk = cut_chunk(v_all, index)
        k_ref[index] = k_chunk.astype(bf16)
        v_ref[index] = v_chunk.astype(bf16)
        for half in range(2):
            keys.append(doubled(k_chunk, half).astype(bf16))
            values.append(doubled(v_chunk, half).astype(bf16))
    mixed = []
    for index in range(CHUNKS):
        q_chunk = turn(cut_chunk(q_all, index), cosine, sine).astype(bf16)
        q_ref[index] = q_chunk
        total = None
        for half in range(2):
            head = 2 * index + half
            if head >= HEADS:
                continue
            s = mm_t(only(q_chunk, half), keys[head // GROUP]) * HEAD_DIM**-0.5
            s = jnp.where(allowed, s, masked_score)
            e = jnp.exp(s - jnp.max(s, axis=-1, keepdims=True))
            p = e / jnp.sum(e, axis=-1, keepdims=True)
            p_ref[head] = p
            part = mm(p.astype(bf16), only(values[head // GROUP], half))
            total = part if total is None else total + part
        mixed.append(total)
    o = jnp.concatenate(mixed, axis=1)[:, :QD].astype(bf16)
    o_ref[...] = o
    o_wide = mm(o, spread).astype(bf16)
    weights.need(1)
    m = h + mm(o_wide, slab(weights, 1))
    m_ref[...] = m
    n2, _ = unit_rows(m)
    b = (n2 * gains_ref[1:2, :]).astype(bf16)
    b_wide = mm(b, spread).astype(bf16)
    hiddens = []
    for piece, (g_ref, u_ref) in enumerate(((g0_ref, u0_ref), (g1_ref, u1_ref), (g2_ref, u2_ref))):
        if piece < 2:
            weights.need(2 + piece)
            weights.need(4 + piece)
        gate = mm(b_wide, gate_slab(weights, piece))
        up = mm(b_wide, up_slab(weights, piece))
        g_ref[...] = gate
        u_ref[...] = up
        hiddens.append((gate * lax.logistic(gate) * up).astype(bf16))
    total = m
    for piece, hidden in enumerate(hiddens):
        weights.need(SLABS + piece)
        total = total + mm(hidden, weights.down_rows(piece))
    y_ref[...] = (total * live_ref[...]).astype(bf16)


def narrow(value, spread):
    high = value.astype(bf16)
    low = (value - high.astype(f32)).astype(bf16)
    both = mm_t(jnp.concatenate([high, low], axis=0), spread)
    return both[: value.shape[0]] + both[value.shape[0] :]


def norm_grad(grad, normal, inverse, gain):
    scaled = grad * gain
    inner = jnp.mean(scaled * normal, axis=-1, keepdims=True)
    return inverse * (scaled - normal * inner)


def feed_forward_back_kernel(
    top_ref, m_ref, live_ref, gains_ref,
    g0_far, g1_far, g2_far, u0_far, u1_far, u2_far, spread_far, big_ref,
    dm_ref, low_ref, d3_ref, dg0_ref, dg1_ref, dg2_ref, du0_ref, du1_ref, du2_ref,
    dgain_ref, b_ref, h0_ref, h1_ref, h2_ref,
    slabs, down, sems,
    g0_ref, g1_ref, g2_ref, u0_ref, u1_ref, u2_ref, spread_ref, near_sems,
):
    far = (g0_far, u0_far, g1_far, u1_far, g2_far, u2_far, spread_far)
    near = (g0_ref, u0_ref, g1_ref, u1_ref, g2_ref, u2_ref, spread_ref)
    brought = [
        pltpu.make_async_copy(source, target, near_sems.at[index])
        for index, (source, target) in enumerate(zip(far, near))
    ]
    for copy in brought[:2]:
        copy.start()
    weights = Loader(big_ref, slabs, down, sems, (8, 2, 4, 9, 3, 5, 10, 6, 7))
    for copy in brought[2:]:
        copy.start()
    gain_f = gains_ref[1:2, :]
    d3 = top_ref[...].astype(f32) * live_ref[...]
    d3_low = d3.astype(bf16)
    d3_ref[...] = d3_low
    n2, r2 = unit_rows(m_ref[...])
    b_ref[...] = (n2 * gain_f).astype(bf16)
    wide = jnp.zeros((d3.shape[0], OWNERS * PADDED), f32)
    refs = (
        (g0_ref, u0_ref, dg0_ref, du0_ref, h0_ref),
        (g1_ref, u1_ref, dg1_ref, du1_ref, h1_ref),
        (g2_ref, u2_ref, dg2_ref, du2_ref, h2_ref),
    )
    for piece, (g_ref, u_ref, dg_ref, du_ref, hid_ref) in enumerate(refs):
        weights.need(SLABS + piece)
        dhidden = mm_t(d3_low, weights.down_rows(piece))
        brought[2 * piece].wait()
        brought[2 * piece + 1].wait()
        gate, up = g_ref[...], u_ref[...]
        sig = lax.logistic(gate)
        act = gate * sig
        hid_ref[...] = (act * up).astype(bf16)
        dg = (dhidden * up * sig * (1.0 + gate * (1.0 - sig))).astype(bf16)
        du = (dhidden * act).astype(bf16)
        dg_ref[...] = dg
        du_ref[...] = du
        if piece < 2:
            weights.need(2 + piece)
            weights.need(4 + piece)
        else:
            weights.need(6)
            weights.need(7)
        wide = wide + mm_t(dg, gate_slab(weights, piece)) + mm_t(du, up_slab(weights, piece))
    brought[6].wait()
    db = narrow(wide, spread_ref[...])
    dgain_ref[...] = jnp.sum(db * n2, axis=0, keepdims=True)
    dm = d3 + norm_grad(db, n2, r2, gain_f)
    dm_ref[...] = dm
    low_ref[...] = dm.astype(bf16)


def attention_back_kernel(
    x_ref, dm_ref, low_ref, q_ref, k_ref, v_ref, p_ref,
    cos_ref, sin_ref, gains_ref, spread_ref, big_ref,
    dh_ref, dq_ref, dk_ref, dv_ref, dgain_ref, a_ref,
    slabs, sems,
):
    weights = Loader(big_ref, slabs, None, sems, (1, 0, 6, 7))
    cosine, sine = cos_ref[...], sin_ref[...]
    spread = spread_ref[...]
    gain_a = gains_ref[0:1, :]
    weights.need(1)
    do = mm_t(mm_t(low_ref[...], slab(weights, 1)).astype(bf16), spread).astype(bf16)
    keys, values = [], []
    for index in range(KV_CHUNKS):
        k_chunk, v_chunk = k_ref[index].astype(f32), v_ref[index].astype(f32)
        for half in range(2):
            keys.append(doubled(k_chunk, half).astype(bf16))
            values.append(doubled(v_chunk, half).astype(bf16))
    dk_sums, dv_sums = [None] * KV_HEADS, [None] * KV_HEADS
    dq_parts = []
    for index in range(CHUNKS):
        do_chunk = cut_chunk(do, index)
        q_chunk = q_ref[index]
        total = None
        for half in range(2):
            head = 2 * index + half
            if head >= HEADS:
                continue
            group = head // GROUP
            do_head, q_head = only(do_chunk, half), only(q_chunk, half)
            p = p_ref[head]
            dp = mm_t(do_head, values[group])
            dv = mm_tl(p.astype(bf16), do_head)
            ds = (p * (dp - jnp.sum(p * dp, axis=-1, keepdims=True))).astype(bf16)
            dk = mm_tl(ds, q_head)
            part = mm(ds, only(keys[group], half))
            total = part if total is None else total + part
            dk_sums[group] = dk if dk_sums[group] is None else dk_sums[group] + dk
            dv_sums[group] = dv if dv_sums[group] is None else dv_sums[group] + dv
        dq_parts.append(turn(total * HEAD_DIM**-0.5, cosine, -sine))
    dq = jnp.concatenate(dq_parts, axis=1)[:, :QD].astype(bf16)
    low_lanes = lanes((do.shape[0], CHUNK)) < HEAD_DIM
    dk_parts, dv_parts = [], []
    for index in range(KV_CHUNKS):
        both = []
        for sums in (dk_sums, dv_sums):
            halves = []
            for half in range(2):
                group = 2 * index + half
                if group < KV_HEADS:
                    halves.append(sums[group] + pltpu.roll(sums[group], HEAD_DIM, 1))
                else:
                    halves.append(jnp.zeros_like(sums[0]))
            both.append(jnp.where(low_lanes, halves[0], halves[1]))
        dk_parts.append(turn(both[0] * HEAD_DIM**-0.5, cosine, -sine))
        dv_parts.append(both[1])
    dk = jnp.concatenate(dk_parts, axis=1)[:, :KVD].astype(bf16)
    dv = jnp.concatenate(dv_parts, axis=1)[:, :KVD].astype(bf16)
    dq_ref[...] = dq
    dk_ref[...] = dk
    dv_ref[...] = dv
    h = x_ref[...].astype(f32)
    n1, r1 = unit_rows(h)
    a_ref[...] = (n1 * gain_a).astype(bf16)
    weights.need(0)
    weights.need(6)
    weights.need(7)
    wide = (
        mm_t(dq, slab(weights, 0))
        + mm_t(dk, slab(weights, 6, 640, 960))
        + mm_t(dv, slab(weights, 7, 640, 960))
    )
    da = narrow(wide, spread)
    dgain_ref[...] = jnp.sum(da * n1, axis=0, keepdims=True)
    dh = dm_ref[...] + norm_grad(da, n1, r1, gain_a)
    dh_ref[...] = dh.astype(bf16)


def takes(microseconds):
    return pl.CostEstimate(
        flops=int(microseconds * 1.1e9), bytes_accessed=int(microseconds * 1e6), transcendentals=0
    )


def specs(count, anywhere=0):
    return [pl.BlockSpec(memory_space=pltpu.VMEM)] * count + [
        pl.BlockSpec(memory_space=pltpu.HBM)
    ] * anywhere


def weight_scratch(slabs):
    return [
        pltpu.VMEM((slabs, OWNERS, PADDED, D), bf16),
        pltpu.VMEM((OWNERS, DOWN_ROWS, D), bf16),
        pltpu.SemaphoreType.DMA((SLABS + len(PIECES),)),
    ]


def shapes(entries):
    return [jax.ShapeDtypeStruct(shape, kind) for shape, kind in entries]


def forward(x, tables, gains, spread, big):
    cosine, sine, allowed, live = tables
    rows = x.shape[0]
    widths = [high - low for low, high in PIECES]
    out = shapes(
        [
            ((rows, D), bf16),
            ((CHUNKS, rows, CHUNK), bf16),
            ((KV_CHUNKS, rows, CHUNK), bf16),
            ((KV_CHUNKS, rows, CHUNK), bf16),
            ((HEADS, rows, rows), f32),
            ((rows, QD), bf16),
            ((rows, D), f32),
        ]
    ) + [pltpu.HBM((rows, width), f32) for width in widths * 2]
    return pl.pallas_call(
        forward_kernel,
        out_shape=out,
        in_specs=specs(7, 1),
        out_specs=specs(len(out)),
        scratch_shapes=weight_scratch(8),
        compiler_params=pltpu.CompilerParams(vmem_limit_bytes=FORWARD_BYTES),
        name="layer_forward",
        cost_estimate=takes(13),
    )(x, cosine, sine, allowed, live, gains, spread, big)


def feed_forward_back(top, saved, tables, gains, spread, big):
    live = tables[3]
    rows = top.shape[0]
    widths = [high - low for low, high in PIECES]
    out = shapes(
        [((rows, D), f32), ((rows, D), bf16), ((rows, D), bf16)]
        + [((rows, width), bf16) for width in widths * 2]
        + [((1, D), f32), ((rows, D), bf16)]
        + [((rows, width), bf16) for width in widths]
    )
    far = [pltpu.with_memory_space_constraint(v, pltpu.HBM) for v in (*saved[6:], spread)]
    return pl.pallas_call(
        feed_forward_back_kernel,
        out_shape=out,
        in_specs=specs(4, 8),
        out_specs=specs(len(out)),
        scratch_shapes=weight_scratch(6)
        + [pltpu.VMEM((rows, width), f32) for width in widths * 2]
        + [pltpu.VMEM(spread.shape, bf16), pltpu.SemaphoreType.DMA((7,))],
        compiler_params=pltpu.CompilerParams(vmem_limit_bytes=FEED_BYTES),
        name="feed_forward_back",
        cost_estimate=takes(14),
    )(top, saved[5], live, gains, *far, big)


def attention_back(x, dm, dm_low, saved, tables, gains, spread, big):
    cosine, sine, _, _ = tables
    rows = x.shape[0]
    out = shapes(
        [((rows, D), bf16), ((rows, QD), bf16), ((rows, KVD), bf16), ((rows, KVD), bf16)]
        + [((1, D), f32), ((rows, D), bf16)]
    )
    scratch = weight_scratch(4)
    return pl.pallas_call(
        attention_back_kernel,
        out_shape=out,
        in_specs=specs(11, 1),
        out_specs=specs(len(out)),
        scratch_shapes=[scratch[0], scratch[2]],
        compiler_params=pltpu.CompilerParams(vmem_limit_bytes=ATTENTION_BYTES),
        name="attention_back",
        cost_estimate=takes(11.5),
    )(x, dm, dm_low, *saved[:4], cosine, sine, gains, spread, big)


def tables_of(starts):
    micro, rows = starts.shape
    local = jnp.arange(rows, dtype=jnp.int32)
    live = (starts <= local).reshape(-1)
    position = jnp.where(starts <= local, local - starts, 0).astype(f32).reshape(-1, 1)
    lane = jnp.arange(CHUNK, dtype=jnp.int32)
    turn_index = (lane % (HEAD_DIM // 2)).astype(f32)
    angles = position * rope_base ** (-2.0 * turn_index / HEAD_DIM)
    sign = jnp.where(lane % HEAD_DIM < HEAD_DIM // 2, -1.0, 1.0).astype(f32)
    row = jnp.arange(micro * rows, dtype=jnp.int32)
    begin = starts.reshape(-1, 1)
    column = row[None, :]
    same = (row[:, None] // rows) == (column // rows)
    inside = (column % rows >= begin) & (column <= row[:, None])
    allowed = (same & inside) | (row[:, None] == column)
    return jnp.cos(angles), jnp.sin(angles) * sign, allowed.astype(f32), live.astype(f32)[:, None]


STREAM_KINDS = (("a",), ("b",), ("b",), ("h0", "h1"), ("o", "h2"))
STREAM_RIGHTS = (14, 20, 20, 8, 16)
STREAM_CHUNKS = (14, 20, 20, 16, 12)
LEFT_ROWS = OWNERS // 2 * PADDED


def rotations(place, then):
    axes = "yzx"
    result = []
    for turned in (axes[start:] + axes[:start] for start in range(3)):
        result.append(
            tuple((axis, place) for axis in turned) + tuple((axis, then) for axis in turned)
        )
    return result


HIGH_FIRST, LOW_FIRST = rotations(1, 0), rotations(0, 1)
ORDERS = (HIGH_FIRST[0], LOW_FIRST[0], LOW_FIRST[1], HIGH_FIRST[1], HIGH_FIRST[2])
GROUPS = ((0, 3, 4), (1, 2))


def split_bit(value, dim, bits):
    shape = value.shape[1:]
    view = value.reshape((2**dim, 2, 2 ** (bits - 1 - dim)) + shape)
    return [view[:, index].reshape((2 ** (bits - 1),) + shape) for index in (0, 1)]


def chunks_of(value):
    count = (value.shape[1] + CHUNK - 1) // CHUNK
    return [cut_chunk(value, index) for index in range(count)]


def write_stream(stream, lefts, rights, keep_ref, pack_ref):
    rows = rights[0].shape[0]
    dim = BITS.index(ORDERS[stream][0])
    base = 0
    for index, left in enumerate(lefts):
        kept, sent = split_bit(left, dim, 6)
        keep_ref[index] = kept
        pack_ref[base : base + LEFT_ROWS, :] = sent.reshape(LEFT_ROWS, rows)
        base += LEFT_ROWS
    for chunk in rights:
        pack_ref[base : base + rows, :] = chunk
        base += rows


def in_order(mine, value):
    return mm_t(mine, value).astype(bf16).reshape(OWNERS, PADDED, value.shape[0])


def gain_table(owned, attn, ffn):
    row = lax.broadcasted_iota(jnp.int32, (D, CHUNK), 0) % SLOT
    lane = lanes((D, CHUNK))
    first = (lane == row).astype(f32).astype(bf16)
    second = (lane == row + SLOT).astype(f32).astype(bf16)
    return mm((owned * attn).astype(bf16), first) + mm((owned * ffn).astype(bf16), second)


def early_operand_kernel(
    mine_ref, b_ref, dg0_ref, dg1_ref, dg2_ref, du0_ref, du1_ref, du2_ref,
    keep1_ref, keep2_ref, pack1_ref, pack2_ref,
):
    b = in_order(mine_ref[...], b_ref[...])
    dg = jnp.concatenate([dg0_ref[...], dg1_ref[...], dg2_ref[...]], axis=1)
    du = jnp.concatenate([du0_ref[...], du1_ref[...], du2_ref[...]], axis=1)
    write_stream(1, (b,), chunks_of(dg), keep1_ref, pack1_ref)
    write_stream(2, (b,), chunks_of(du), keep2_ref, pack2_ref)


def late_operand_kernel(
    owner_ref, mine_ref, owned_ref, a_ref, o_ref, h0_ref, h1_ref, h2_ref, dm_ref, d3_ref,
    attn_ref, ffn_ref, dq_ref, dk_ref, dv_ref,
    *rest,
):
    keeps, packs = rest[:3], rest[3:6]
    turned, lefts = rest[6:]
    mine = mine_ref[...]
    rows = a_ref.shape[0]

    table = gain_table(owned_ref[...], attn_ref[...], ffn_ref[...])
    a = mm_t(mine, a_ref[...]).reshape(OWNERS, PADDED, rows)
    spare = lax.broadcasted_iota(jnp.int32, a.shape, 1) == SLOT
    a = jnp.where(spare, table[:, None, :], a).astype(bf16)
    dq, dk, dv = dq_ref[...], dk_ref[...], dv_ref[...]
    tail = jnp.concatenate([dq[:, 896:], dk[:, 256:]], axis=1)
    identity = lax.broadcasted_iota(jnp.int32, (rows, CHUNK), 0) == lanes((rows, CHUNK))
    rights = chunks_of(dq)[:7] + chunks_of(dk)[:2] + [tail] + chunks_of(dv)
    rights.append(identity.astype(f32).astype(bf16))
    write_stream(0, (a,), rights, keeps[0], packs[0])

    hidden = jnp.concatenate([h0_ref[...], h1_ref[...], h2_ref[...]], axis=1).astype(f32)
    turned[...] = hidden.T.reshape(OWNERS, DOWN_ROWS, rows)

    @pl.loop(0, OWNERS)
    def _(place):
        block = turned[owner_ref[place]]
        lefts[0, place] = block[0:16].astype(bf16)
        lefts[1, place] = block[16:32].astype(bf16)
        lefts[2, place] = jnp.concatenate(
            [block[32:40], jnp.zeros((8, rows), f32)], axis=0
        ).astype(bf16)

    d3, dm = chunks_of(d3_ref[...]), chunks_of(dm_ref[...])
    o = in_order(mine, o_ref[...])
    write_stream(3, (lefts[0], lefts[1]), d3, keeps[1], packs[1])
    write_stream(4, (o, lefts[2]), dm + d3, keeps[2], packs[2])


def operand_shapes(streams, rows):
    return shapes(
        [((len(STREAM_KINDS[s]), OWNERS // 2, PADDED, rows), bf16) for s in streams]
        + [
            ((len(STREAM_KINDS[s]) * LEFT_ROWS + STREAM_RIGHTS[s] * rows, CHUNK), bf16)
            for s in streams
        ]
    )


def early_operands(mine, b, dg, du):
    result = pl.pallas_call(
        early_operand_kernel,
        out_shape=operand_shapes((1, 2), b.shape[0]),
        in_specs=specs(8),
        out_specs=specs(4),
        compiler_params=pltpu.CompilerParams(vmem_limit_bytes=VMEM_BYTES),
        name="early_operands",
        cost_estimate=takes(2),
    )(mine, b, *dg, *du)
    return result[:2], result[2:]


def late_operands(owners, mine, owned, a, o, hidden, dm_low, d3, dattn, dffn, dq, dk, dv):
    rows = a.shape[0]
    result = pl.pallas_call(
        late_operand_kernel,
        out_shape=operand_shapes((0, 3, 4), rows),
        in_specs=[pl.BlockSpec(memory_space=pltpu.SMEM)] + specs(14),
        out_specs=specs(6),
        scratch_shapes=[
            pltpu.VMEM((OWNERS, DOWN_ROWS, rows), f32),
            pltpu.VMEM((3, OWNERS, PADDED, rows), bf16),
        ],
        compiler_params=pltpu.CompilerParams(vmem_limit_bytes=VMEM_BYTES),
        name="late_operands",
        cost_estimate=takes(3),
    )(owners, mine, owned, a, o, *hidden, dm_low, d3, dattn, dffn, dq, dk, dv)
    return result[:3], result[3:]


def product_kernel(streams, *refs):
    count = len(streams)
    keeps, packs, others = (
        dict(zip(streams, refs[count * part : count * (part + 1)])) for part in range(3)
    )
    outs = {s: refs[3 * count + 2 * i : 3 * count + 2 * i + 2] for i, s in enumerate(streams)}
    step = pl.program_id(0)

    def left_of(stream, kind):
        kept = keeps[stream][kind].reshape(LEFT_ROWS, CHUNK)
        window = pl.ds(kind * LEFT_ROWS, LEFT_ROWS)
        return jnp.concatenate([kept, others[stream][window, :]], axis=1)

    def right_of(stream, chunk):
        start = len(STREAM_KINDS[stream]) * LEFT_ROWS + chunk * CHUNK
        if not isinstance(start, int):
            start = pl.multiple_of(start, CHUNK)
        window = pl.ds(start, CHUNK)
        return jnp.concatenate([packs[stream][window, :], others[stream][window, :]], axis=0)

    def right_pair(stream, first, second):
        return jnp.concatenate([right_of(stream, first), right_of(stream, second)], axis=1)

    def blocks_of(value):
        return value.reshape(OWNERS // 2, PADDED, CHUNK)

    def store(stream, place, value):
        dim = [bit for bit in BITS if bit != ORDERS[stream][0]].index(ORDERS[stream][1])
        kept, sent = split_bit(value.astype(bf16), dim, 5)
        outs[stream][0][place] = kept
        outs[stream][1][place] = sent

    def usual(stream, kind, first):
        value = mm(left_of(stream, kind), right_pair(stream, first, first + 1))
        store(stream, 0, blocks_of(value[:, :CHUNK]))
        store(stream, 1, blocks_of(value[:, CHUNK:]))

    def short_rows(stream, kind, first):
        value = mm(left_of(stream, kind), right_pair(stream, first, first + 4))
        parts = [blocks_of(part)[:, :8] for part in (value[:, :CHUNK], value[:, CHUNK:])]
        return jnp.concatenate(parts, axis=1)

    def when(condition, action):
        pl.when(condition)(action)

    if 0 in streams:
        when(step < 7, lambda: usual(0, 0, 2 * step))
    if 1 in streams:
        usual(1, 0, 2 * step)
    if 2 in streams:
        usual(2, 0, 2 * step)
    if 3 in streams:
        when(step < 4, lambda: usual(3, 0, 2 * step))
        when(step >= 4, lambda: usual(3, 1, 2 * step - 8))
    if 4 in streams:
        when(step < 4, lambda: usual(4, 0, 2 * step))

        @pl.when((step >= 4) & (step < 6))
        def _():
            for place in range(2):
                store(4, place, short_rows(4, 1, 8 + 2 * (step - 4) + place))


def products(streams, keeps, packs, others):
    out, out_specs = [], []
    for stream in streams:
        last = STREAM_CHUNKS[stream] // 2 - 1
        for _ in range(2):
            out.append(((STREAM_CHUNKS[stream], OWNERS // 4, PADDED, CHUNK), bf16))
            out_specs.append(
                pl.BlockSpec(
                    (2, OWNERS // 4, PADDED, CHUNK),
                    lambda step, last=last: (jnp.minimum(step, last), 0, 0, 0),
                )
            )
    result = pl.pallas_call(
        partial(product_kernel, streams),
        grid=(max(STREAM_CHUNKS[stream] for stream in streams) // 2,),
        out_shape=shapes(out),
        in_specs=specs(3 * len(streams)),
        out_specs=out_specs,
        compiler_params=pltpu.CompilerParams(vmem_limit_bytes=VMEM_BYTES),
        name="grad_products",
        cost_estimate=takes(sum(STREAM_CHUNKS[stream] for stream in streams) * 0.2),
    )(*keeps, *packs, *others)
    return list(result[0::2]), list(result[1::2])


def together(values):
    return list(lax.optimization_barrier(tuple(values)))


def send(values, bits):
    return together([lax.ppermute(v, "dp", partner_pairs(b)) for v, b in zip(values, bits)])


def halved(kept, arrived, dim):
    size = kept.shape[1]
    view = (kept.shape[0], 2**dim, 2, size >> (dim + 1)) + kept.shape[2:]
    flat = (kept.shape[0], size // 2) + kept.shape[2:]
    first, second = kept.reshape(view), arrived.reshape(view)
    return tuple(
        (first[:, :, index].astype(f32) + second[:, :, index].astype(f32))
        .astype(bf16)
        .reshape(flat)
        for index in (0, 1)
    )


def exchanged(streams, packs):
    return [
        lax.ppermute(pack, "dp", partner_pairs(ORDERS[stream][0]))
        for stream, pack in zip(streams, packs)
    ]


def three_steps(streams, keeps, packs, others):
    orders = [ORDERS[stream] for stream in streams]
    kept, sent = products(streams, keeps, packs, others)
    arrived = send(sent, [order[1] for order in orders])
    for index, order in enumerate(orders):
        left = [bit for bit in BITS if bit not in order[:2]]
        kept[index], sent[index] = halved(kept[index], arrived[index], left.index(order[2]))
    return kept, send(sent, [order[2] for order in orders])


def last_steps(parts):
    kept, sent, rest = [], [], []
    for members, (keeps, arrived) in zip(GROUPS, parts):
        order = ORDERS[members[0]]
        left = [bit for bit in BITS if bit not in order[:3]]
        halves = [halved(k, a, left.index(order[3])) for k, a in zip(keeps, arrived)]
        kept.append(jnp.concatenate([half[0] for half in halves], axis=0))
        sent.append(jnp.concatenate([half[1] for half in halves], axis=0))
        rest.append((left, order[3:]))
    for step in range(3):
        arrived = send(sent, [order[step] for _, order in rest])
        for group, (left, order) in enumerate(rest):
            left.remove(order[step])
            if step < 2:
                dim = left.index(order[step + 1])
                kept[group], sent[group] = halved(kept[group], arrived[group], dim)
    return kept, arrived


def result_kernel(
    kept0_ref, kept1_ref, came0_ref, came1_ref,
    query_ref, key_ref, value_ref, output_ref, gate_ref, up_ref, down_ref, attn_ref, ffn_ref,
):
    def block(group, index):
        kept, came = ((kept0_ref, came0_ref), (kept1_ref, came1_ref))[group]
        return kept[index, 0].astype(f32) + came[index, 0].astype(f32)

    def put(ref, low, high, value, column):
        width = min(CHUNK, ref.shape[-1] - column)
        value = value[: high - low, :width]
        if len(ref.shape) == 3:
            ref[low:high, 0, column : column + width] = value
        else:
            ref[low:high, column : column + width] = value

    half = HEAD_DIM
    for index in range(7):
        put(query_ref, 0, SLOT, block(0, index), CHUNK * index)
    for index in range(2):
        put(key_ref, 0, SLOT, block(0, 7 + index), CHUNK * index)
    tail = block(0, 9)
    put(query_ref, 0, SLOT, tail, 896)
    put(key_ref, 0, SLOT, tail[:, half:], 256)
    for index in range(3):
        put(value_ref, 0, SLOT, block(0, 10 + index), CHUNK * index)
    gains = block(0, 13)[SLOT:]
    attn_ref[...] = gains[:, :SLOT]
    ffn_ref[...] = gains[:, SLOT : 2 * SLOT]
    for index in range(8):
        put(down_ref, 0, 16, block(0, 14 + index), CHUNK * index)
        put(down_ref, 16, 32, block(0, 22 + index), CHUNK * index)
        put(output_ref, 0, SLOT, block(0, 30 + index), CHUNK * index)
    for index in range(4):
        both = block(0, 38 + index)
        put(down_ref, 32, 40, both[:8], CHUNK * index)
        put(down_ref, 32, 40, both[8:], CHUNK * (index + 4))
    for index in range(20):
        put(gate_ref, 0, SLOT, block(1, index), CHUNK * index)
        put(up_ref, 0, SLOT, block(1, 20 + index), CHUNK * index)


def weight_results(kept, came):
    wide = [(SLOT, 1, width) for width in (QD, KVD, KVD, D, FF, FF)]
    out = shapes([(shape, f32) for shape in wide + [(DOWN_ROWS, D), (1, SLOT), (1, SLOT)]])
    result = pl.pallas_call(
        result_kernel,
        out_shape=out,
        in_specs=specs(4),
        out_specs=specs(len(out)),
        name="weight_results",
        cost_estimate=takes(3),
    )(*kept, *came)
    slots = tuple(value.transpose(1, 0, 2) for value in result[:6])
    return slots + (result[6][None],) + tuple(result[7:])


def pack_kernel(q_ref, k_ref, v_ref, o_ref, g_ref, u_ref, d_ref, gain_ref, out_ref):
    blank = jnp.zeros((PADDED - SLOT, D), bf16)
    g, u = g_ref[0], u_ref[0]
    plain = (
        q_ref[0],
        o_ref[0],
        g[:, :960],
        g[:, 960:1920],
        u[:, :960],
        u[:, 960:1920],
        jnp.concatenate([g[:, 1920:], k_ref[0]], axis=1),
        jnp.concatenate([u[:, 1920:], v_ref[0]], axis=1),
    )
    for index, value in enumerate(plain):
        last = gain_ref[...] if index == 0 else blank
        full = jnp.concatenate([value.astype(f32), last.astype(f32)], axis=0)
        out_ref[0, PADDED * index : PADDED * (index + 1), :] = full.astype(bf16)
    out_ref[0, PADDED * SLABS :, :] = d_ref[0]


def packed_weights(w_query, w_key, w_value, w_output, w_gate, w_up, w_down, attn_gain, ffn_gain):
    gains = jnp.concatenate([attn_gain, ffn_gain], axis=1)
    gain_row = jnp.pad(gains, ((0, 0), (0, D - gains.shape[1])))
    return pl.pallas_call(
        pack_kernel,
        out_shape=jax.ShapeDtypeStruct((1, PADDED * SLABS + DOWN_ROWS, D), bf16),
        in_specs=specs(8),
        out_specs=pl.BlockSpec(memory_space=pltpu.VMEM),
        name="pack_weights",
        cost_estimate=takes(2),
    )(w_query, w_key, w_value, w_output, w_gate, w_up, w_down, gain_row)


def body(inputs, starts, cotangent, *weights):
    section = lax.axis_index("section")
    micro, rows = starts.shape
    everything = lax.all_gather(packed_weights(*weights), "dp", axis=0, tiled=True)
    owners = owner_of(jnp.arange(OWNERS, dtype=jnp.int32))
    owned = (jnp.arange(D, dtype=jnp.int32) // SLOT == owners[:, None]).astype(f32)
    everything, spread, mine, owners, owned, *tables = together(
        [everything, spread_matrix(), own_spread(), owners, owned, *tables_of(starts)]
    )
    all_gains = everything[:, SLOT, : 2 * SLOT].astype(f32)
    all_gains = jnp.stack([all_gains[:, :SLOT].reshape(D), all_gains[:, SLOT:].reshape(D)])
    first_in = inputs.reshape(micro * rows, D)
    top = cotangent.reshape(micro * rows, D)
    everything = pltpu.with_memory_space_constraint(everything, pltpu.HBM)
    shared = (tables, all_gains, spread, everything)

    made = forward(first_in, *shared)[0]
    arrived = lax.ppermute(made, "section", [(0, 1)])
    source = jnp.where(section == 0, first_in, arrived)
    result, *saved = forward(source, *shared)

    dm, dm_low = feed_forward_back(top, saved, *shared)[:2]
    back = attention_back(source, dm, dm_low, saved, *shared)[0]
    returned = lax.ppermute(back, "section", [(1, 0)])
    upstream = jnp.where(section == 1, top, returned)

    ffn = feed_forward_back(upstream, saved, *shared)
    dm, dm_low, d3, dffn, b, hidden = ffn[0], ffn[1], ffn[2], ffn[9], ffn[10], ffn[11:14]
    keeps, packs = early_operands(mine, b, ffn[3:6], ffn[6:9])
    dm, dm_low, *packs = together([dm, dm_low, *packs])
    others = exchanged((1, 2), packs)
    grad_rows, dq, dk, dv, dattn, a = attention_back(source, dm, dm_low, saved, *shared)
    late_keeps, late_packs = late_operands(
        owners, mine, owned, a, saved[4], hidden, dm_low, d3, dattn, dffn, dq, dk, dv
    )
    *late_packs, other1, other2 = together([*late_packs, *others])
    query_pack, down_pack, output_pack = late_packs
    query_other, down_other, output_other = exchanged((0, 3, 4), late_packs)

    gate_up = three_steps((1, 2), keeps, packs, [other1, other2])
    query_down = three_steps(
        (0, 3), late_keeps[:2], [query_pack, down_pack], [query_other, down_other]
    )
    output = three_steps((4,), late_keeps[2:], [output_pack], [output_other])
    first_group = (query_down[0] + output[0], query_down[1] + output[1])
    sums = weight_results(*last_steps((first_group, gate_up)))
    rows_out = (result.reshape(1, micro, rows, D), grad_rows.reshape(1, micro, rows, D))
    return rows_out + sums


def solution(mesh):
    split = P("section", "dp", None)
    return jax.shard_map(
        body,
        mesh=mesh,
        in_specs=(P(None, "dp", None), P(None, "dp"), P(None, "dp", None))
        + (split,) * 7
        + (P("section", "dp"),) * 2,
        out_specs=(P("section", None, "dp", None),) * 2
        + (split,) * 7
        + (P("section", "dp"),) * 2,
        check_vma=False,
    )
```

```python
from functools import partial

import jax
import jax.numpy as jnp
from jax import lax
from jax.experimental import pallas as pl
from jax.experimental.pallas import tpu as pltpu
from jax.sharding import PartitionSpec as P

D = 960
HEADS = 15
KV_HEADS = 5
GROUP = HEADS // KV_HEADS
HEAD_DIM = 64
FF = 2560
QD = 960
KVD = 320
OWNERS = 64
SLOT = 15
PADDED = 16
DOWN_ROWS = 40

norm_eps = 1e-05
masked_score = -1e30
rope_base = 10000.0

f32 = jnp.float32
bf16 = jnp.bfloat16


def gray(value):
    return value ^ (value >> 1)


AXIS_SHIFT = {"y": 4, "z": 2, "x": 0}
BITS = (("y", 1), ("y", 0), ("z", 1), ("z", 0), ("x", 1), ("x", 0))


def partner_pairs(bit):
    axis, place = bit
    shift = AXIS_SHIFT[axis]
    pairs = []
    for source in range(OWNERS):
        coordinate = (source >> shift) & 3
        other = gray(gray(coordinate) ^ (1 << place))
        pairs.append((source, source + ((other - coordinate) << shift)))
    return pairs


def owner_of(position):
    me = lax.axis_index("dp")
    owner = 0
    for shift in (4, 2, 0):
        owner = owner + (gray(gray((me >> shift) & 3) ^ ((position >> shift) & 3)) << shift)
    return owner


def dot(left, right):
    return jnp.dot(left, right, preferred_element_type=f32)


def dot_t(left, right):
    return lax.dot_general(left, right, (((1,), (1,)), ((), ())), preferred_element_type=f32)


def spread_matrix():
    row = lax.broadcasted_iota(jnp.int32, (D, OWNERS * PADDED), 0)
    col = lax.broadcasted_iota(jnp.int32, (D, OWNERS * PADDED), 1)
    return ((row == SLOT * (col // PADDED) + col % PADDED) & (col % PADDED < SLOT)).astype(bf16)


def own_spread():
    row = lax.broadcasted_iota(jnp.int32, (OWNERS * PADDED, D), 0)
    col = lax.broadcasted_iota(jnp.int32, (OWNERS * PADDED, D), 1)
    owner = owner_of(row // PADDED)
    return ((col == SLOT * owner + row % PADDED) & (row % PADDED < SLOT)).astype(bf16)


CHUNK = 128
CHUNKS = 8
KV_CHUNKS = 3
PIECES = ((0, 960), (960, 1920), (1920, 2560))
SLABS = 8
VMEM_BYTES = 20 * 2**20
FORWARD_BYTES = 34 * 2**20
FEED_BYTES = 36 * 2**20
ATTENTION_BYTES = 20 * 2**20


def mm(left, right):
    return lax.dot_general(left, right, (((1,), (0,)), ((), ())), preferred_element_type=f32)


def mm_t(left, right):
    return lax.dot_general(left, right, (((1,), (1,)), ((), ())), preferred_element_type=f32)


def mm_tl(left, right):
    return lax.dot_general(left, right, (((0,), (0,)), ((), ())), preferred_element_type=f32)


def lanes(shape):
    return lax.broadcasted_iota(jnp.int32, shape, len(shape) - 1)


def cut_chunk(value, index):
    width = value.shape[1]
    low = index * CHUNK
    high = min(low + CHUNK, width)
    part = value[:, low:high]
    if high - low < CHUNK:
        part = jnp.concatenate(
            [part, jnp.zeros((value.shape[0], CHUNK - (high - low)), value.dtype)], axis=1
        )
    return part


def turn(value, cosine, sine):
    first = lanes(value.shape) % HEAD_DIM < HEAD_DIM // 2
    swapped = jnp.where(
        first, pltpu.roll(value, CHUNK - HEAD_DIM // 2, 1), pltpu.roll(value, HEAD_DIM // 2, 1)
    )
    return value * cosine + swapped * sine


def doubled(chunk, half):
    other = pltpu.roll(chunk, HEAD_DIM, 1)
    low = lanes(chunk.shape) < HEAD_DIM
    return jnp.where(low, chunk, other) if half == 0 else jnp.where(low, other, chunk)


def only(chunk, half):
    keep = (lanes(chunk.shape) < HEAD_DIM) == (half == 0)
    return jnp.where(keep, chunk, jnp.zeros_like(chunk))


class Loader:
    def __init__(self, big_ref, slabs, down, sems, order):
        self.slabs, self.down, self.copies = slabs, down, {}
        self.places = {index: place for place, index in enumerate(i for i in order if i < SLABS)}
        for index in order:
            if index < SLABS:
                source = big_ref.at[:, pl.ds(PADDED * index, PADDED), :]
                target = slabs.at[self.places[index]]
            else:
                low, high = (bound // DOWN_ROWS for bound in PIECES[index - SLABS])
                source = big_ref.at[low:high, PADDED * SLABS :, :]
                target = down.at[low:high]
            self.copies[index] = pltpu.make_async_copy(source, target, sems.at[index])
            self.copies[index].start()

    def need(self, index):
        self.copies[index].wait()

    def __getitem__(self, index):
        return self.slabs[self.places[index]]

    def down_rows(self, piece):
        low, high = PIECES[piece]
        return self.down[low // DOWN_ROWS : high // DOWN_ROWS].reshape(high - low, D)


def slab(slabs, index, low=0, high=D):
    return slabs[index].reshape(OWNERS * PADDED, D)[:, low:high]


def gate_slab(slabs, piece):
    return slab(slabs, 2 + piece) if piece < 2 else slab(slabs, 6, 0, 640)


def up_slab(slabs, piece):
    return slab(slabs, 4 + piece) if piece < 2 else slab(slabs, 7, 0, 640)


def unit_rows(value):
    inverse = lax.rsqrt(jnp.mean(value * value, axis=-1, keepdims=True) + norm_eps)
    return value * inverse, inverse


def forward_kernel(
    x_ref, cos_ref, sin_ref, allow_ref, live_ref, gains_ref, spread_ref, big_ref,
    y_ref, q_ref, k_ref, v_ref, p_ref, o_ref, m_ref, g0_ref, g1_ref, g2_ref, u0_ref, u1_ref, u2_ref,
    slabs, down, sems,
):
    weights = Loader(big_ref, slabs, down, sems, (0, 6, 7, 1, 2, 4, 3, 5, 8, 9, 10))
    cosine, sine = cos_ref[...], sin_ref[...]
    allowed = allow_ref[...] > 0
    spread = spread_ref[...]
    h = x_ref[...].astype(f32)
    n1, _ = unit_rows(h)
    a = (n1 * gains_ref[0:1, :]).astype(bf16)
    a_wide = mm(a, spread).astype(bf16)
    weights.need(0)
    q_all = mm(a_wide, slab(weights, 0))
    weights.need(6)
    k_all = mm(a_wide, slab(weights, 6, 640, 960))
    weights.need(7)
    v_all = mm(a_wide, slab(weights, 7, 640, 960))
    keys, values = [], []
    for index in range(KV_CHUNKS):
        k_chunk = turn(cut_chunk(k_all, index), cosine, sine)
        v_chunk = cut_chunk(v_all, index)
        k_ref[index] = k_chunk.astype(bf16)
        v_ref[index] = v_chunk.astype(bf16)
        for half in range(2):
            keys.append(doubled(k_chunk, half).astype(bf16))
            values.append(doubled(v_chunk, half).astype(bf16))
    mixed = []
    for index in range(CHUNKS):
        q_chunk = turn(cut_chunk(q_all, index), cosine, sine).astype(bf16)
        q_ref[index] = q_chunk
        total = None
        for half in range(2):
            head = 2 * index + half
            if head >= HEADS:
                continue
            s = mm_t(only(q_chunk, half), keys[head // GROUP]) * HEAD_DIM**-0.5
            s = jnp.where(allowed, s, masked_score)
            e = jnp.exp(s - jnp.max(s, axis=-1, keepdims=True))
            p = e / jnp.sum(e, axis=-1, keepdims=True)
            p_ref[head] = p
            part = mm(p.astype(bf16), only(values[head // GROUP], half))
            total = part if total is None else total + part
        mixed.append(total)
    o = jnp.concatenate(mixed, axis=1)[:, :QD].astype(bf16)
    o_ref[...] = o
    o_wide = mm(o, spread).astype(bf16)
    weights.need(1)
    m = h + mm(o_wide, slab(weights, 1))
    m_ref[...] = m
    n2, _ = unit_rows(m)
    b = (n2 * gains_ref[1:2, :]).astype(bf16)
    b_wide = mm(b, spread).astype(bf16)
    hiddens = []
    for piece, (g_ref, u_ref) in enumerate(((g0_ref, u0_ref), (g1_ref, u1_ref), (g2_ref, u2_ref))):
        if piece < 2:
            weights.need(2 + piece)
            weights.need(4 + piece)
        gate = mm(b_wide, gate_slab(weights, piece))
        up = mm(b_wide, up_slab(weights, piece))
        g_ref[...] = gate
        u_ref[...] = up
        hiddens.append((gate * lax.logistic(gate) * up).astype(bf16))
    total = m
    for piece, hidden in enumerate(hiddens):
        weights.need(SLABS + piece)
        total = total + mm(hidden, weights.down_rows(piece))
    y_ref[...] = (total * live_ref[...]).astype(bf16)


def narrow(value, spread):
    high = value.astype(bf16)
    low = (value - high.astype(f32)).astype(bf16)
    both = mm_t(jnp.concatenate([high, low], axis=0), spread)
    return both[: value.shape[0]] + both[value.shape[0] :]


def norm_grad(grad, normal, inverse, gain):
    scaled = grad * gain
    inner = jnp.mean(scaled * normal, axis=-1, keepdims=True)
    return inverse * (scaled - normal * inner)


def feed_forward_back_kernel(
    top_ref, m_ref, live_ref, gains_ref,
    g0_far, g1_far, g2_far, u0_far, u1_far, u2_far, spread_far, big_ref,
    dm_ref, low_ref, d3_ref, dg0_ref, dg1_ref, dg2_ref, du0_ref, du1_ref, du2_ref,
    dgain_ref, b_ref, h0_ref, h1_ref, h2_ref,
    slabs, down, sems,
    g0_ref, g1_ref, g2_ref, u0_ref, u1_ref, u2_ref, spread_ref, near_sems,
):
    far = (g0_far, u0_far, g1_far, u1_far, g2_far, u2_far, spread_far)
    near = (g0_ref, u0_ref, g1_ref, u1_ref, g2_ref, u2_ref, spread_ref)
    brought = [
        pltpu.make_async_copy(source, target, near_sems.at[index])
        for index, (source, target) in enumerate(zip(far, near))
    ]
    for copy in brought[:2]:
        copy.start()
    weights = Loader(big_ref, slabs, down, sems, (8, 2, 4, 9, 3, 5, 10, 6, 7))
    for copy in brought[2:]:
        copy.start()
    gain_f = gains_ref[1:2, :]
    d3 = top_ref[...].astype(f32) * live_ref[...]
    d3_low = d3.astype(bf16)
    d3_ref[...] = d3_low
    n2, r2 = unit_rows(m_ref[...])
    b_ref[...] = (n2 * gain_f).astype(bf16)
    wide = jnp.zeros((d3.shape[0], OWNERS * PADDED), f32)
    refs = (
        (g0_ref, u0_ref, dg0_ref, du0_ref, h0_ref),
        (g1_ref, u1_ref, dg1_ref, du1_ref, h1_ref),
        (g2_ref, u2_ref, dg2_ref, du2_ref, h2_ref),
    )
    for piece, (g_ref, u_ref, dg_ref, du_ref, hid_ref) in enumerate(refs):
        weights.need(SLABS + piece)
        dhidden = mm_t(d3_low, weights.down_rows(piece))
        brought[2 * piece].wait()
        brought[2 * piece + 1].wait()
        gate, up = g_ref[...], u_ref[...]
        sig = lax.logistic(gate)
        act = gate * sig
        hid_ref[...] = (act * up).astype(bf16)
        dg = (dhidden * up * sig * (1.0 + gate * (1.0 - sig))).astype(bf16)
        du = (dhidden * act).astype(bf16)
        dg_ref[...] = dg
        du_ref[...] = du
        if piece < 2:
            weights.need(2 + piece)
            weights.need(4 + piece)
        else:
            weights.need(6)
            weights.need(7)
        wide = wide + mm_t(dg, gate_slab(weights, piece)) + mm_t(du, up_slab(weights, piece))
    brought[6].wait()
    db = narrow(wide, spread_ref[...])
    dgain_ref[...] = jnp.sum(db * n2, axis=0, keepdims=True)
    dm = d3 + norm_grad(db, n2, r2, gain_f)
    dm_ref[...] = dm
    low_ref[...] = dm.astype(bf16)


def attention_back_kernel(
    x_ref, dm_ref, low_ref, q_ref, k_ref, v_ref, p_ref,
    cos_ref, sin_ref, gains_ref, spread_ref, big_ref,
    dh_ref, dq_ref, dk_ref, dv_ref, dgain_ref, a_ref,
    slabs, sems,
):
    weights = Loader(big_ref, slabs, None, sems, (1, 0, 6, 7))
    cosine, sine = cos_ref[...], sin_ref[...]
    spread = spread_ref[...]
    gain_a = gains_ref[0:1, :]
    weights.need(1)
    do = mm_t(mm_t(low_ref[...], slab(weights, 1)).astype(bf16), spread).astype(bf16)
    keys, values = [], []
    for index in range(KV_CHUNKS):
        k_chunk, v_chunk = k_ref[index].astype(f32), v_ref[index].astype(f32)
        for half in range(2):
            keys.append(doubled(k_chunk, half).astype(bf16))
            values.append(doubled(v_chunk, half).astype(bf16))
    dk_sums, dv_sums = [None] * KV_HEADS, [None] * KV_HEADS
    dq_parts = []
    for index in range(CHUNKS):
        do_chunk = cut_chunk(do, index)
        q_chunk = q_ref[index]
        total = None
        for half in range(2):
            head = 2 * index + half
            if head >= HEADS:
                continue
            group = head // GROUP
            do_head, q_head = only(do_chunk, half), only(q_chunk, half)
            p = p_ref[head]
            dp = mm_t(do_head, values[group])
            dv = mm_tl(p.astype(bf16), do_head)
            ds = (p * (dp - jnp.sum(p * dp, axis=-1, keepdims=True))).astype(bf16)
            dk = mm_tl(ds, q_head)
            part = mm(ds, only(keys[group], half))
            total = part if total is None else total + part
            dk_sums[group] = dk if dk_sums[group] is None else dk_sums[group] + dk
            dv_sums[group] = dv if dv_sums[group] is None else dv_sums[group] + dv
        dq_parts.append(turn(total * HEAD_DIM**-0.5, cosine, -sine))
    dq = jnp.concatenate(dq_parts, axis=1)[:, :QD].astype(bf16)
    low_lanes = lanes((do.shape[0], CHUNK)) < HEAD_DIM
    dk_parts, dv_parts = [], []
    for index in range(KV_CHUNKS):
        both = []
        for sums in (dk_sums, dv_sums):
            halves = []
            for half in range(2):
                group = 2 * index + half
                if group < KV_HEADS:
                    halves.append(sums[group] + pltpu.roll(sums[group], HEAD_DIM, 1))
                else:
                    halves.append(jnp.zeros_like(sums[0]))
            both.append(jnp.where(low_lanes, halves[0], halves[1]))
        dk_parts.append(turn(both[0] * HEAD_DIM**-0.5, cosine, -sine))
        dv_parts.append(both[1])
    dk = jnp.concatenate(dk_parts, axis=1)[:, :KVD].astype(bf16)
    dv = jnp.concatenate(dv_parts, axis=1)[:, :KVD].astype(bf16)
    dq_ref[...] = dq
    dk_ref[...] = dk
    dv_ref[...] = dv
    h = x_ref[...].astype(f32)
    n1, r1 = unit_rows(h)
    a_ref[...] = (n1 * gain_a).astype(bf16)
    weights.need(0)
    weights.need(6)
    weights.need(7)
    wide = (
        mm_t(dq, slab(weights, 0))
        + mm_t(dk, slab(weights, 6, 640, 960))
        + mm_t(dv, slab(weights, 7, 640, 960))
    )
    da = narrow(wide, spread)
    dgain_ref[...] = jnp.sum(da * n1, axis=0, keepdims=True)
    dh = dm_ref[...] + norm_grad(da, n1, r1, gain_a)
    dh_ref[...] = dh.astype(bf16)


def takes(microseconds):
    return pl.CostEstimate(
        flops=int(microseconds * 1.1e9), bytes_accessed=int(microseconds * 1e6), transcendentals=0
    )


def specs(count, anywhere=0):
    return [pl.BlockSpec(memory_space=pltpu.VMEM)] * count + [
        pl.BlockSpec(memory_space=pltpu.HBM)
    ] * anywhere


def weight_scratch(slabs):
    return [
        pltpu.VMEM((slabs, OWNERS, PADDED, D), bf16),
        pltpu.VMEM((OWNERS, DOWN_ROWS, D), bf16),
        pltpu.SemaphoreType.DMA((SLABS + len(PIECES),)),
    ]


def shapes(entries):
    return [jax.ShapeDtypeStruct(shape, kind) for shape, kind in entries]


def forward(x, tables, gains, spread, big):
    cosine, sine, allowed, live = tables
    rows = x.shape[0]
    widths = [high - low for low, high in PIECES]
    out = shapes(
        [
            ((rows, D), bf16),
            ((CHUNKS, rows, CHUNK), bf16),
            ((KV_CHUNKS, rows, CHUNK), bf16),
            ((KV_CHUNKS, rows, CHUNK), bf16),
            ((HEADS, rows, rows), f32),
            ((rows, QD), bf16),
            ((rows, D), f32),
        ]
    ) + [pltpu.HBM((rows, width), f32) for width in widths * 2]
    return pl.pallas_call(
        forward_kernel,
        out_shape=out,
        in_specs=specs(7, 1),
        out_specs=specs(len(out)),
        scratch_shapes=weight_scratch(8),
        compiler_params=pltpu.CompilerParams(vmem_limit_bytes=FORWARD_BYTES),
        name="layer_forward",
        cost_estimate=takes(13),
    )(x, cosine, sine, allowed, live, gains, spread, big)


def feed_forward_back(top, saved, tables, gains, spread, big):
    live = tables[3]
    rows = top.shape[0]
    widths = [high - low for low, high in PIECES]
    out = shapes(
        [((rows, D), f32), ((rows, D), bf16), ((rows, D), bf16)]
        + [((rows, width), bf16) for width in widths * 2]
        + [((1, D), f32), ((rows, D), bf16)]
        + [((rows, width), bf16) for width in widths]
    )
    far = [pltpu.with_memory_space_constraint(v, pltpu.HBM) for v in (*saved[6:], spread)]
    return pl.pallas_call(
        feed_forward_back_kernel,
        out_shape=out,
        in_specs=specs(4, 8),
        out_specs=specs(len(out)),
        scratch_shapes=weight_scratch(6)
        + [pltpu.VMEM((rows, width), f32) for width in widths * 2]
        + [pltpu.VMEM(spread.shape, bf16), pltpu.SemaphoreType.DMA((7,))],
        compiler_params=pltpu.CompilerParams(vmem_limit_bytes=FEED_BYTES),
        name="feed_forward_back",
        cost_estimate=takes(14),
    )(top, saved[5], live, gains, *far, big)


def attention_back(x, dm, dm_low, saved, tables, gains, spread, big):
    cosine, sine, _, _ = tables
    rows = x.shape[0]
    out = shapes(
        [((rows, D), bf16), ((rows, QD), bf16), ((rows, KVD), bf16), ((rows, KVD), bf16)]
        + [((1, D), f32), ((rows, D), bf16)]
    )
    scratch = weight_scratch(4)
    return pl.pallas_call(
        attention_back_kernel,
        out_shape=out,
        in_specs=specs(11, 1),
        out_specs=specs(len(out)),
        scratch_shapes=[scratch[0], scratch[2]],
        compiler_params=pltpu.CompilerParams(vmem_limit_bytes=ATTENTION_BYTES),
        name="attention_back",
        cost_estimate=takes(11.5),
    )(x, dm, dm_low, *saved[:4], cosine, sine, gains, spread, big)


def tables_of(starts):
    micro, rows = starts.shape
    local = jnp.arange(rows, dtype=jnp.int32)
    live = (starts <= local).reshape(-1)
    position = jnp.where(starts <= local, local - starts, 0).astype(f32).reshape(-1, 1)
    lane = jnp.arange(CHUNK, dtype=jnp.int32)
    turn_index = (lane % (HEAD_DIM // 2)).astype(f32)
    angles = position * rope_base ** (-2.0 * turn_index / HEAD_DIM)
    sign = jnp.where(lane % HEAD_DIM < HEAD_DIM // 2, -1.0, 1.0).astype(f32)
    row = jnp.arange(micro * rows, dtype=jnp.int32)
    begin = starts.reshape(-1, 1)
    column = row[None, :]
    same = (row[:, None] // rows) == (column // rows)
    inside = (column % rows >= begin) & (column <= row[:, None])
    allowed = (same & inside) | (row[:, None] == column)
    return jnp.cos(angles), jnp.sin(angles) * sign, allowed.astype(f32), live.astype(f32)[:, None]


STREAM_KINDS = (("a",), ("b",), ("b",), ("h0", "h1"), ("o", "h2"))
STREAM_RIGHTS = (14, 20, 20, 8, 16)
STREAM_CHUNKS = (14, 20, 20, 16, 12)
LEFT_ROWS = OWNERS // 2 * PADDED


def rotations(place, then):
    axes = "yzx"
    result = []
    for turned in (axes[start:] + axes[:start] for start in range(3)):
        result.append(
            tuple((axis, place) for axis in turned) + tuple((axis, then) for axis in turned)
        )
    return result


HIGH_FIRST, LOW_FIRST = rotations(1, 0), rotations(0, 1)
ORDERS = (HIGH_FIRST[0], LOW_FIRST[0], LOW_FIRST[1], HIGH_FIRST[1], HIGH_FIRST[2])
GROUPS = ((0, 3, 4), (1, 2))


def split_bit(value, dim, bits):
    shape = value.shape[1:]
    view = value.reshape((2**dim, 2, 2 ** (bits - 1 - dim)) + shape)
    return [view[:, index].reshape((2 ** (bits - 1),) + shape) for index in (0, 1)]


def chunks_of(value):
    count = (value.shape[1] + CHUNK - 1) // CHUNK
    return [cut_chunk(value, index) for index in range(count)]


def write_stream(stream, lefts, rights, keep_ref, pack_ref):
    rows = rights[0].shape[0]
    dim = BITS.index(ORDERS[stream][0])
    base = 0
    for index, left in enumerate(lefts):
        kept, sent = split_bit(left, dim, 6)
        keep_ref[index] = kept
        pack_ref[base : base + LEFT_ROWS, :] = sent.reshape(LEFT_ROWS, rows)
        base += LEFT_ROWS
    for chunk in rights:
        pack_ref[base : base + rows, :] = chunk
        base += rows


def in_order(mine, value):
    return mm_t(mine, value).astype(bf16).reshape(OWNERS, PADDED, value.shape[0])


def gain_table(owned, attn, ffn):
    row = lax.broadcasted_iota(jnp.int32, (D, CHUNK), 0) % SLOT
    lane = lanes((D, CHUNK))
    first = (lane == row).astype(f32).astype(bf16)
    second = (lane == row + SLOT).astype(f32).astype(bf16)
    return mm((owned * attn).astype(bf16), first) + mm((owned * ffn).astype(bf16), second)


def early_operand_kernel(
    mine_ref, b_ref, dg0_ref, dg1_ref, dg2_ref, du0_ref, du1_ref, du2_ref,
    keep1_ref, keep2_ref, pack1_ref, pack2_ref,
):
    b = in_order(mine_ref[...], b_ref[...])
    dg = jnp.concatenate([dg0_ref[...], dg1_ref[...], dg2_ref[...]], axis=1)
    du = jnp.concatenate([du0_ref[...], du1_ref[...], du2_ref[...]], axis=1)
    write_stream(1, (b,), chunks_of(dg), keep1_ref, pack1_ref)
    write_stream(2, (b,), chunks_of(du), keep2_ref, pack2_ref)


def late_operand_kernel(
    owner_ref, mine_ref, owned_ref, a_ref, o_ref, h0_ref, h1_ref, h2_ref, dm_ref, d3_ref,
    attn_ref, ffn_ref, dq_ref, dk_ref, dv_ref,
    *rest,
):
    keeps, packs = rest[:3], rest[3:6]
    turned, lefts = rest[6:]
    mine = mine_ref[...]
    rows = a_ref.shape[0]

    table = gain_table(owned_ref[...], attn_ref[...], ffn_ref[...])
    a = mm_t(mine, a_ref[...]).reshape(OWNERS, PADDED, rows)
    spare = lax.broadcasted_iota(jnp.int32, a.shape, 1) == SLOT
    a = jnp.where(spare, table[:, None, :], a).astype(bf16)
    dq, dk, dv = dq_ref[...], dk_ref[...], dv_ref[...]
    tail = jnp.concatenate([dq[:, 896:], dk[:, 256:]], axis=1)
    identity = lax.broadcasted_iota(jnp.int32, (rows, CHUNK), 0) == lanes((rows, CHUNK))
    rights = chunks_of(dq)[:7] + chunks_of(dk)[:2] + [tail] + chunks_of(dv)
    rights.append(identity.astype(f32).astype(bf16))
    write_stream(0, (a,), rights, keeps[0], packs[0])

    hidden = jnp.concatenate([h0_ref[...], h1_ref[...], h2_ref[...]], axis=1).astype(f32)
    turned[...] = hidden.T.reshape(OWNERS, DOWN_ROWS, rows)

    @pl.loop(0, OWNERS)
    def _(place):
        block = turned[owner_ref[place]]
        lefts[0, place] = block[0:16].astype(bf16)
        lefts[1, place] = block[16:32].astype(bf16)
        lefts[2, place] = jnp.concatenate(
            [block[32:40], jnp.zeros((8, rows), f32)], axis=0
        ).astype(bf16)

    d3, dm = chunks_of(d3_ref[...]), chunks_of(dm_ref[...])
    o = in_order(mine, o_ref[...])
    write_stream(3, (lefts[0], lefts[1]), d3, keeps[1], packs[1])
    write_stream(4, (o, lefts[2]), dm + d3, keeps[2], packs[2])


def operand_shapes(streams, rows):
    return shapes(
        [((len(STREAM_KINDS[s]), OWNERS // 2, PADDED, rows), bf16) for s in streams]
        + [
            ((len(STREAM_KINDS[s]) * LEFT_ROWS + STREAM_RIGHTS[s] * rows, CHUNK), bf16)
            for s in streams
        ]
    )


def early_operands(mine, b, dg, du):
    result = pl.pallas_call(
        early_operand_kernel,
        out_shape=operand_shapes((1, 2), b.shape[0]),
        in_specs=specs(8),
        out_specs=specs(4),
        compiler_params=pltpu.CompilerParams(vmem_limit_bytes=VMEM_BYTES),
        name="early_operands",
        cost_estimate=takes(2),
    )(mine, b, *dg, *du)
    return result[:2], result[2:]


def late_operands(owners, mine, owned, a, o, hidden, dm_low, d3, dattn, dffn, dq, dk, dv):
    rows = a.shape[0]
    result = pl.pallas_call(
        late_operand_kernel,
        out_shape=operand_shapes((0, 3, 4), rows),
        in_specs=[pl.BlockSpec(memory_space=pltpu.SMEM)] + specs(14),
        out_specs=specs(6),
        scratch_shapes=[
            pltpu.VMEM((OWNERS, DOWN_ROWS, rows), f32),
            pltpu.VMEM((3, OWNERS, PADDED, rows), bf16),
        ],
        compiler_params=pltpu.CompilerParams(vmem_limit_bytes=VMEM_BYTES),
        name="late_operands",
        cost_estimate=takes(3),
    )(owners, mine, owned, a, o, *hidden, dm_low, d3, dattn, dffn, dq, dk, dv)
    return result[:3], result[3:]


def product_kernel(streams, *refs):
    count = len(streams)
    keeps, packs, others = (
        dict(zip(streams, refs[count * part : count * (part + 1)])) for part in range(3)
    )
    outs = {s: refs[3 * count + 2 * i : 3 * count + 2 * i + 2] for i, s in enumerate(streams)}
    step = pl.program_id(0)

    def left_of(stream, kind):
        kept = keeps[stream][kind].reshape(LEFT_ROWS, CHUNK)
        window = pl.ds(kind * LEFT_ROWS, LEFT_ROWS)
        return jnp.concatenate([kept, others[stream][window, :]], axis=1)

    def right_of(stream, chunk):
        start = len(STREAM_KINDS[stream]) * LEFT_ROWS + chunk * CHUNK
        if not isinstance(start, int):
            start = pl.multiple_of(start, CHUNK)
        window = pl.ds(start, CHUNK)
        return jnp.concatenate([packs[stream][window, :], others[stream][window, :]], axis=0)

    def right_pair(stream, first, second):
        return jnp.concatenate([right_of(stream, first), right_of(stream, second)], axis=1)

    def blocks_of(value):
        return value.reshape(OWNERS // 2, PADDED, CHUNK)

    def store(stream, place, value):
        dim = [bit for bit in BITS if bit != ORDERS[stream][0]].index(ORDERS[stream][1])
        kept, sent = split_bit(value.astype(bf16), dim, 5)
        outs[stream][0][place] = kept
        outs[stream][1][place] = sent

    def usual(stream, kind, first):
        value = mm(left_of(stream, kind), right_pair(stream, first, first + 1))
        store(stream, 0, blocks_of(value[:, :CHUNK]))
        store(stream, 1, blocks_of(value[:, CHUNK:]))

    def short_rows(stream, kind, first):
        value = mm(left_of(stream, kind), right_pair(stream, first, first + 4))
        parts = [blocks_of(part)[:, :8] for part in (value[:, :CHUNK], value[:, CHUNK:])]
        return jnp.concatenate(parts, axis=1)

    def when(condition, action):
        pl.when(condition)(action)

    if 0 in streams:
        when(step < 7, lambda: usual(0, 0, 2 * step))
    if 1 in streams:
        usual(1, 0, 2 * step)
    if 2 in streams:
        usual(2, 0, 2 * step)
    if 3 in streams:
        when(step < 4, lambda: usual(3, 0, 2 * step))
        when(step >= 4, lambda: usual(3, 1, 2 * step - 8))
    if 4 in streams:
        when(step < 4, lambda: usual(4, 0, 2 * step))

        @pl.when((step >= 4) & (step < 6))
        def _():
            for place in range(2):
                store(4, place, short_rows(4, 1, 8 + 2 * (step - 4) + place))


def products(streams, keeps, packs, others):
    out, out_specs = [], []
    for stream in streams:
        last = STREAM_CHUNKS[stream] // 2 - 1
        for _ in range(2):
            out.append(((STREAM_CHUNKS[stream], OWNERS // 4, PADDED, CHUNK), bf16))
            out_specs.append(
                pl.BlockSpec(
                    (2, OWNERS // 4, PADDED, CHUNK),
                    lambda step, last=last: (jnp.minimum(step, last), 0, 0, 0),
                )
            )
    result = pl.pallas_call(
        partial(product_kernel, streams),
        grid=(max(STREAM_CHUNKS[stream] for stream in streams) // 2,),
        out_shape=shapes(out),
        in_specs=specs(3 * len(streams)),
        out_specs=out_specs,
        compiler_params=pltpu.CompilerParams(vmem_limit_bytes=VMEM_BYTES),
        name="grad_products",
        cost_estimate=takes(sum(STREAM_CHUNKS[stream] for stream in streams) * 0.6),
    )(*keeps, *packs, *others)
    return list(result[0::2]), list(result[1::2])


def together(values):
    return list(lax.optimization_barrier(tuple(values)))


def send(values, bits):
    return together([lax.ppermute(v, "dp", partner_pairs(b)) for v, b in zip(values, bits)])


def halved(kept, arrived, dim):
    size = kept.shape[1]
    view = (kept.shape[0], 2**dim, 2, size >> (dim + 1)) + kept.shape[2:]
    flat = (kept.shape[0], size // 2) + kept.shape[2:]
    first, second = kept.reshape(view), arrived.reshape(view)
    return tuple(
        (first[:, :, index].astype(f32) + second[:, :, index].astype(f32))
        .astype(bf16)
        .reshape(flat)
        for index in (0, 1)
    )


def exchanged(streams, packs):
    return [
        lax.ppermute(pack, "dp", partner_pairs(ORDERS[stream][0]))
        for stream, pack in zip(streams, packs)
    ]


def three_steps(streams, keeps, packs, others):
    orders = [ORDERS[stream] for stream in streams]
    kept, sent = products(streams, keeps, packs, others)
    arrived = send(sent, [order[1] for order in orders])
    for index, order in enumerate(orders):
        left = [bit for bit in BITS if bit not in order[:2]]
        kept[index], sent[index] = halved(kept[index], arrived[index], left.index(order[2]))
    return kept, send(sent, [order[2] for order in orders])


def last_steps(parts):
    kept, sent, rest = [], [], []
    for members, (keeps, arrived) in zip(GROUPS, parts):
        order = ORDERS[members[0]]
        left = [bit for bit in BITS if bit not in order[:3]]
        halves = [halved(k, a, left.index(order[3])) for k, a in zip(keeps, arrived)]
        kept.append(jnp.concatenate([half[0] for half in halves], axis=0))
        sent.append(jnp.concatenate([half[1] for half in halves], axis=0))
        rest.append((left, order[3:]))
    for step in range(3):
        arrived = send(sent, [order[step] for _, order in rest])
        for group, (left, order) in enumerate(rest):
            left.remove(order[step])
            if step < 2:
                dim = left.index(order[step + 1])
                kept[group], sent[group] = halved(kept[group], arrived[group], dim)
    return kept, arrived


def result_kernel(
    kept0_ref, kept1_ref, came0_ref, came1_ref,
    query_ref, key_ref, value_ref, output_ref, gate_ref, up_ref, down_ref, attn_ref, ffn_ref,
):
    def block(group, index):
        kept, came = ((kept0_ref, came0_ref), (kept1_ref, came1_ref))[group]
        return kept[index, 0].astype(f32) + came[index, 0].astype(f32)

    def put(ref, low, high, value, column):
        width = min(CHUNK, ref.shape[-1] - column)
        value = value[: high - low, :width]
        if len(ref.shape) == 3:
            ref[low:high, 0, column : column + width] = value
        else:
            ref[low:high, column : column + width] = value

    half = HEAD_DIM
    for index in range(7):
        put(query_ref, 0, SLOT, block(0, index), CHUNK * index)
    for index in range(2):
        put(key_ref, 0, SLOT, block(0, 7 + index), CHUNK * index)
    tail = block(0, 9)
    put(query_ref, 0, SLOT, tail, 896)
    put(key_ref, 0, SLOT, tail[:, half:], 256)
    for index in range(3):
        put(value_ref, 0, SLOT, block(0, 10 + index), CHUNK * index)
    gains = block(0, 13)[SLOT:]
    attn_ref[...] = gains[:, :SLOT]
    ffn_ref[...] = gains[:, SLOT : 2 * SLOT]
    for index in range(8):
        put(down_ref, 0, 16, block(0, 14 + index), CHUNK * index)
        put(down_ref, 16, 32, block(0, 22 + index), CHUNK * index)
        put(output_ref, 0, SLOT, block(0, 30 + index), CHUNK * index)
    for index in range(4):
        both = block(0, 38 + index)
        put(down_ref, 32, 40, both[:8], CHUNK * index)
        put(down_ref, 32, 40, both[8:], CHUNK * (index + 4))
    for index in range(20):
        put(gate_ref, 0, SLOT, block(1, index), CHUNK * index)
        put(up_ref, 0, SLOT, block(1, 20 + index), CHUNK * index)


def weight_results(kept, came):
    wide = [(SLOT, 1, width) for width in (QD, KVD, KVD, D, FF, FF)]
    out = shapes([(shape, f32) for shape in wide + [(DOWN_ROWS, D), (1, SLOT), (1, SLOT)]])
    result = pl.pallas_call(
        result_kernel,
        out_shape=out,
        in_specs=specs(4),
        out_specs=specs(len(out)),
        name="weight_results",
        cost_estimate=takes(3),
    )(*kept, *came)
    slots = tuple(value.transpose(1, 0, 2) for value in result[:6])
    return slots + (result[6][None],) + tuple(result[7:])


def pack_kernel(q_ref, k_ref, v_ref, o_ref, g_ref, u_ref, d_ref, gain_ref, out_ref):
    blank = jnp.zeros((PADDED - SLOT, D), bf16)
    g, u = g_ref[0], u_ref[0]
    plain = (
        q_ref[0],
        o_ref[0],
        g[:, :960],
        g[:, 960:1920],
        u[:, :960],
        u[:, 960:1920],
        jnp.concatenate([g[:, 1920:], k_ref[0]], axis=1),
        jnp.concatenate([u[:, 1920:], v_ref[0]], axis=1),
    )
    for index, value in enumerate(plain):
        last = gain_ref[...] if index == 0 else blank
        full = jnp.concatenate([value.astype(f32), last.astype(f32)], axis=0)
        out_ref[0, PADDED * index : PADDED * (index + 1), :] = full.astype(bf16)
    out_ref[0, PADDED * SLABS :, :] = d_ref[0]


def packed_weights(w_query, w_key, w_value, w_output, w_gate, w_up, w_down, attn_gain, ffn_gain):
    gains = jnp.concatenate([attn_gain, ffn_gain], axis=1)
    gain_row = jnp.pad(gains, ((0, 0), (0, D - gains.shape[1])))
    return pl.pallas_call(
        pack_kernel,
        out_shape=jax.ShapeDtypeStruct((1, PADDED * SLABS + DOWN_ROWS, D), bf16),
        in_specs=specs(8),
        out_specs=pl.BlockSpec(memory_space=pltpu.VMEM),
        name="pack_weights",
        cost_estimate=takes(2),
    )(w_query, w_key, w_value, w_output, w_gate, w_up, w_down, gain_row)


def body(inputs, starts, cotangent, *weights):
    section = lax.axis_index("section")
    micro, rows = starts.shape
    everything = lax.all_gather(packed_weights(*weights), "dp", axis=0, tiled=True)
    owners = owner_of(jnp.arange(OWNERS, dtype=jnp.int32))
    owned = (jnp.arange(D, dtype=jnp.int32) // SLOT == owners[:, None]).astype(f32)
    everything, spread, mine, owners, owned, *tables = together(
        [everything, spread_matrix(), own_spread(), owners, owned, *tables_of(starts)]
    )
    all_gains = everything[:, SLOT, : 2 * SLOT].astype(f32)
    all_gains = jnp.stack([all_gains[:, :SLOT].reshape(D), all_gains[:, SLOT:].reshape(D)])
    first_in = inputs.reshape(micro * rows, D)
    top = cotangent.reshape(micro * rows, D)
    everything = pltpu.with_memory_space_constraint(everything, pltpu.HBM)
    shared = (tables, all_gains, spread, everything)

    made = forward(first_in, *shared)[0]
    arrived = lax.ppermute(made, "section", [(0, 1)])
    source = jnp.where(section == 0, first_in, arrived)
    result, *saved = forward(source, *shared)

    dm, dm_low = feed_forward_back(top, saved, *shared)[:2]
    back = attention_back(source, dm, dm_low, saved, *shared)[0]
    returned = lax.ppermute(back, "section", [(1, 0)])
    upstream = jnp.where(section == 1, top, returned)

    ffn = feed_forward_back(upstream, saved, *shared)
    dm, dm_low, d3, dffn, b, hidden = ffn[0], ffn[1], ffn[2], ffn[9], ffn[10], ffn[11:14]
    keeps, packs = early_operands(mine, b, ffn[3:6], ffn[6:9])
    dm, dm_low, *packs = together([dm, dm_low, *packs])
    others = exchanged((1, 2), packs)
    grad_rows, dq, dk, dv, dattn, a = attention_back(source, dm, dm_low, saved, *shared)
    late_keeps, late_packs = late_operands(
        owners, mine, owned, a, saved[4], hidden, dm_low, d3, dattn, dffn, dq, dk, dv
    )
    *late_packs, other1, other2 = together([*late_packs, *others])
    query_pack, down_pack, output_pack = late_packs
    query_other, down_other, output_other = exchanged((0, 3, 4), late_packs)

    gate_up = three_steps((1, 2), keeps, packs, [other1, other2])
    query_down = three_steps(
        (0, 3), late_keeps[:2], [query_pack, down_pack], [query_other, down_other]
    )
    output = three_steps((4,), late_keeps[2:], [output_pack], [output_other])
    first_group = (query_down[0] + output[0], query_down[1] + output[1])
    sums = weight_results(*last_steps((first_group, gate_up)))
    rows_out = (result.reshape(1, micro, rows, D), grad_rows.reshape(1, micro, rows, D))
    return rows_out + sums


def solution(mesh):
    split = P("section", "dp", None)
    return jax.shard_map(
        body,
        mesh=mesh,
        in_specs=(P(None, "dp", None), P(None, "dp"), P(None, "dp", None))
        + (split,) * 7
        + (P("section", "dp"),) * 2,
        out_specs=(P("section", None, "dp", None),) * 2
        + (split,) * 7
        + (P("section", "dp"),) * 2,
        check_vma=False,
    )
```
